512 devices in a mesh: tm: 32 (over y, x), tile: 16 (over z, core).
Axes of the slice: x: 4, y: 8, z: 8, core: 2. Of those that a mesh axis runs over, the one named last changes fastest.
Arguments:
- prior: float32 [512, 512], P('tile'), may hold values from -1 to 7, as said below
- station_nodes: int32 [32, 2048, 3], P('tm', 'tile'), may hold values from 0 to 511
- station_weights: float32 [32, 2048, 3], P('tm', 'tile'), may hold values from 0.1 to 1
- station_counts: int32 [32, 2048], P('tm', 'tile'), may hold values from 0 to 8
- modes: float32 [32, 512, 32], P('tm'), may hold values from -1 to 1
- data: float32 [32, 512, 128], P('tm'), may hold values from -6 to 6
- kappa: float32 [16], P('tile'), may hold values from 0.7 to 1.4
- tau: float32 [16], P('tile'), may hold values from 0.01 to 0.1
- rho: float32 [16], P('tile'), may hold values from 0.24 to 0.99
Outputs:
- solution: float32 [32, 16, 512, 128], P('tm', 'tile')
- mean_logdet: float32 [16], P('tile')
The draws below stay inside these ranges and needn't reach their ends.
Inputs may be any that keep to these rules, and one draw needn't show every extreme that they name: `prior`: symmetric and positive definite; rho[c] <= 0.985 kappa[c] / 1.4 for every configuration, so that every configuration's block-tridiagonal precision is positive definite.
All inputs are finite; a program needn't handle non-finite values.
Results may differ from the reference program's by a relative error of at most 0.0003.
Values sent between devices are 32-bit elements; how exact they have to be, the bound alone decides.
No kernel may reach another device: no remote copies, remote signals or barrier semaphores. Data moves between devices by JAX's collectives and lax.ppermute only.
A program may use at most 64 MiB of HBM per device.

```python
import math
import jax
import jax.numpy as jnp
from jax import lax

NS = 512
R = 32
NRHS = 128
NT = 32
CONF = 16
STATIONS = 2048


def prior_root(key):
    first_key, second_key = jax.random.split(jax.random.fold_in(key, 11))
    diagonal_values = jax.random.uniform(first_key, (NS,), jnp.float32, 1.6, 2.4)
    spread = 0.7 / NS ** 0.5
    noise = jax.random.uniform(second_key, (NS, NS), jnp.float32, -spread, spread)
    return 0.5 * (noise + noise.T) + jnp.diag(diagonal_values)


def draw_prior(key, part):
    root = prior_root(key)
    square = jnp.dot(root, root, precision=lax.Precision.HIGHEST)
    return 0.5 * (square + square.T)


def draw_modes(key, part):
    root = prior_root(key)
    sign_key, order_key = jax.random.split(jax.random.fold_in(key, 23))
    signs = (2 * jax.random.randint(sign_key, (NT, NS), 0, 2) - 1).astype(jnp.float32)
    order_keys = jax.random.split(order_key, NT)
    orders = jax.vmap(lambda single: jax.random.permutation(single, NS))(order_keys)
    owners = orders % R
    selector = (owners[:, :, None] == jnp.arange(R)[None, None, :]).astype(jnp.float32)
    magnitude = (0.7 * R / NS) ** 0.5
    sparse_basis = selector * signs[:, :, None] * magnitude
    return jnp.einsum('ij,tjr->tir', root, sparse_basis, precision=lax.Precision.HIGHEST)


def kappa_values(key):
    level = jax.random.uniform(jax.random.fold_in(key, 41), (CONF,), jnp.float32, 0.0, 1.0)
    return jnp.exp(jnp.log(0.7) + level * jnp.log(2.0))


def draw_kappa(key, part):
    return kappa_values(key)


def draw_rho(key, part):
    rate_key = jax.random.fold_in(key, 37)
    strength = jax.random.uniform(rate_key, (CONF,), jnp.float32, 0.5, 0.985)
    return strength * kappa_values(key) / 1.4


def touch_ends(result, own_key, low, high):
    longest = result.shape.index(max(result.shape))
    spots = []
    for shift in (0, 1):
        where = [jax.random.randint(jax.random.fold_in(own_key, axis), (), 0, length) for axis, length in enumerate(result.shape)]
        where[longest] = (where[longest] + shift) % result.shape[longest]
        spots.append(tuple(where))
    return result.at[spots[0]].set(low).at[spots[1]].set(high)


def level_of(rng, dims, shards, least, top_value):
    def one(position, shards_of):
        draws = jax.random.uniform(jax.random.fold_in(jax.random.fold_in(rng, 6), position), (shards_of,), jnp.float32, least / len(shards), top_value / len(shards))
        return jnp.repeat(jnp.exp(draws), dims[position] // shards_of).reshape((-1,) + (1,) * (len(dims) - position - 1))

    loudness = one(*shards[0])
    for cut in shards[1:]:
        loudness = loudness * one(*cut)
    return loudness


def scatter_about(stream_key, dims, scale, most, cuts=(), dtype=jnp.bfloat16):
    gain = level_of(stream_key, dims, cuts, -0.22, 0.18) if cuts else 1.0
    drawn = jax.random.normal(stream_key, dims, jnp.float32) * scale * gain
    return jnp.minimum(jnp.maximum(drawn, -most), most).astype(dtype)


def setup_inputs(seed: int = 0) -> dict:
    seeds = jax.random.split(jax.random.key(seed), 10)
    return {
        "prior": draw_prior(jax.random.fold_in(seeds[9], 71), 0),
        "station_nodes": touch_ends(jax.random.randint(seeds[1], (NT, STATIONS, 3), 0, NS), jax.random.fold_in(seeds[1], 1), 0, NS - 1).astype(jnp.int32),
        "station_weights": jnp.clip(0.1 + 0.9 * jax.random.uniform(seeds[2], (NT, STATIONS, 3), jnp.float32) ** level_of(seeds[2], (NT, STATIONS, 3), ((0, 32), (1, 16)), -0.2, 0.2), 0.1, 1.0),
        "station_counts": touch_ends(jax.random.randint(seeds[3], (NT, STATIONS), 0, 9), jax.random.fold_in(seeds[3], 1), 0, 8).astype(jnp.int32),
        "modes": draw_modes(jax.random.fold_in(seeds[9], 71), 0),
        "data": scatter_about(seeds[5], (NT, NS, NRHS), 1.0, 6.0, ((0, 32),), jnp.float32),
        "kappa": draw_kappa(jax.random.fold_in(seeds[9], 71), 0),
        "tau": jnp.clip(jnp.exp(math.log(0.1) - 2.3025851 * jax.random.uniform(seeds[7], (CONF,), jnp.float32) ** level_of(seeds[7], (CONF,), ((0, 16),), -0.2, 0.2)), 0.01, 0.1),
        "rho": draw_rho(jax.random.fold_in(seeds[9], 71), 0),
    }


PRECISE = lax.Precision.HIGHEST

def matmul(left, right):
    return jnp.dot(left, right, precision=PRECISE)

def solve_spd(factor, right):
    first_half = lax.linalg.triangular_solve(factor, right, left_side=True, lower=True)
    return lax.linalg.triangular_solve(factor, first_half, left_side=True, lower=True, transpose_a=True)

def gram_matrix(nodes, weights, counts):
    terms = counts.astype(jnp.float32)[:, None, None] * weights[:, :, None] * weights[:, None, :]
    stations = nodes.shape[0]
    row_index = jnp.broadcast_to(nodes[:, :, None], (stations, 3, 3)).reshape(stations * 9).astype(jnp.int32)
    column_index = jnp.broadcast_to(nodes[:, None, :], (stations, 3, 3)).reshape(stations * 9).astype(jnp.int32)
    empty = jnp.zeros((NS, NS), jnp.float32)
    return empty.at[row_index, column_index].add(terms.reshape(stations * 9))

def reference(prior, station_nodes, station_weights, station_counts, modes, data, kappa, tau, rho):

    def one_config(params):
        scale_prior, observed_scale, coupling = params

        def forward(carry, inputs):
            incoming, loads_in, total = carry
            nodes, weights, counts, basis, right_sides = inputs
            block = scale_prior * prior + observed_scale * gram_matrix(nodes, weights, counts)
            coupled = coupling * basis
            schur = block - matmul(matmul(coupled, incoming), coupled.T)
            factor = jnp.linalg.cholesky(schur)
            loads = right_sides + matmul(coupled, loads_in)
            solved = solve_spd(factor, jnp.concatenate([basis, loads], axis=1))
            solved_modes = solved[:, :R]
            solved_loads = solved[:, R:]
            outgoing = matmul(basis.T, solved_modes)
            loads_out = matmul(basis.T, solved_loads)
            total = total + 2.0 * jnp.sum(jnp.log(jnp.diagonal(factor)))
            return ((outgoing, loads_out, total), (solved_modes, solved_loads))
        start = (jnp.zeros((R, R), jnp.float32), jnp.zeros((R, NRHS), jnp.float32), jnp.zeros((), jnp.float32))
        finals, solved_all = lax.scan(forward, start, (station_nodes, station_weights, station_counts, modes, data))
        total = finals[2]

        def backward(reply, inputs):
            solved_modes, solved_loads, basis = inputs
            field = solved_loads + coupling * matmul(solved_modes, reply)
            return (matmul(basis.T, field), field)
        unused, fields = lax.scan(backward, jnp.zeros((R, NRHS), jnp.float32), (solved_all[0], solved_all[1], modes), reverse=True)
        return (fields, total / (NT * NS))
    fields, logdets = lax.map(one_config, (kappa, tau, rho))
    return (jnp.transpose(fields, (1, 0, 2, 3)), logdets)
```

```python
import jax
import jax.numpy as jnp
from jax import lax
from jax.experimental import pallas as pl
from jax.experimental.pallas import tpu as pltpu
from jax.sharding import PartitionSpec as P

f32 = jnp.float32
bf16 = jnp.bfloat16
NN = ((1,), (0,))
NT = ((1,), (1,))
TN = ((0,), (0,))
SEG = 32


def dot(a, b, dims=NN, precision=lax.Precision.HIGHEST):
    return lax.dot_general(a, b, (dims, ((), ())), precision=precision, preferred_element_type=f32)


def iotas():
    return (
        lax.broadcasted_iota(jnp.int32, (8, 128), 0),
        lax.broadcasted_iota(jnp.int32, (8, 128), 1),
    )


def row_of(v, k):
    return jnp.broadcast_to(v[k : k + 1, :], v.shape)


def inverse(rows, width):
    sub, lane = iotas()
    local = lane % width
    first = lane - local
    groups = width // 8
    logs = jnp.zeros((8, 128), f32)
    rows = list(rows)
    for b in range(groups):
        start = 8 * b
        pivots = (local >= start) & (local < start + 8)

        def column(tile, k):
            if width == 128:
                return jnp.broadcast_to(tile[:, start + k : start + k + 1], tile.shape)
            return jnp.take_along_axis(tile, first + (start + k), axis=1)

        columns = [[column(rows[g], k) for k in range(8)] for g in range(groups)]
        own = list(columns[b])
        panel = jnp.where(pivots, jnp.where(local - start == sub, 1.0, 0.0), rows[b])
        scale = jnp.ones((8, 128), f32)
        for k in range(8):
            inv = 1.0 / row_of(own[k], k)
            factor = jnp.where(sub == k, 0.0, own[k] * inv)
            scale = jnp.where(sub == k, inv, scale)
            for m in range(k + 1, 8):
                own[m] = own[m] - factor * row_of(own[m], k)
            panel = panel - factor * row_of(panel, k)
        panel = panel * scale
        logs = logs - jnp.log(scale)
        spread = [row_of(panel, k) for k in range(8)]
        for g in range(groups):
            if g != b:
                t = [columns[g][k] * spread[k] for k in range(8)]
                total = ((t[0] + t[1]) + (t[2] + t[3])) + ((t[4] + t[5]) + (t[6] + t[7]))
                rows[g] = jnp.where(pivots, 0.0, rows[g]) - total
        rows[b] = panel
    return rows, logs


def factor_kernel(kappa_ref, tau_ref, near_ref, far_ref, modes_ref, data_ref, x_ref, send_ref,
                  work_ref, high_ref, low_ref, inv_ref):
    step = lax.axis_index("tm")
    nodes, ranks = modes_ref.shape
    cols = data_ref.shape[1]
    chips = near_ref.shape[0]
    parts = 2 * chips
    core = lax.axis_index("tile") % 2
    band = nodes // parts
    tiles = nodes // 128
    kappa = kappa_ref[0]
    tau = tau_ref[0]
    ids = lax.broadcasted_iota(jnp.int32, (nodes, 128), 0).astype(f32)
    for p in range(parts):
        s = (near_ref if p < chips else far_ref)[p % chips, tiles * band :, :]
        n0, n1, n2, w0, w1, w2 = [s[i : i + 1] for i in range(6)]
        root = jnp.sqrt(s[6:7])
        same01 = n1 == n0
        same02 = n2 == n0
        same12 = (n2 == n1) & jnp.logical_not(same02)
        w0 = w0 + jnp.where(same01, w1, 0.0) + jnp.where(same02, w2, 0.0)
        w1 = w1 + jnp.where(same12, w2, 0.0)
        w0, w1, w2 = w0 * root, w1 * root, w2 * root
        h0, h1, h2 = [w.astype(bf16).astype(f32) for w in (w0, w1, w2)]
        m0, m1, m2 = ids == n0, ids == n1, ids == n2

        def place(a, b, c):
            return jnp.where(m0, a, jnp.where(m1, b, jnp.where(m2, c, 0.0))).astype(bf16)

        at = slice(p * 128, (p + 1) * 128)
        high_ref[:, at] = place(h0, h1, h2)
        low_ref[:, at] = place(w0 - h0, w1 - h1, w2 - h2)
    half = nodes // 2
    for i in range(2):
        rs = slice(i * half, (i + 1) * half)
        high = high_ref[rs, :]
        gram = (dot(high, high_ref[...], NT, None) + dot(high, low_ref[...], NT, None)
                + dot(low_ref[rs, :], high_ref[...], NT, None))
        work_ref[rs, :nodes] = tau * gram
    for ref, side in ((near_ref, core), (far_ref, 1 - core)):
        for p in range(chips):
            at = pl.ds(pl.multiple_of((2 * p + side) * band, band), band)
            for c in range(tiles):
                cs = slice(c * 128, (c + 1) * 128)
                work_ref[at, cs] = work_ref[at, cs] + kappa * ref[p, c * band : (c + 1) * band, :]
    work_ref[:, nodes : nodes + cols] = data_ref[...]
    basis = modes_ref[...]
    work_ref[:, nodes + cols :] = jnp.concatenate([basis] * (128 // ranks), axis=1)
    width = nodes + cols + 128
    logs = jnp.zeros((8, 128), f32)
    for k in range(tiles):
        rs = slice(128 * k, 128 * (k + 1))
        rows, more = inverse([work_ref[128 * k + 8 * g : 128 * k + 8 * g + 8, rs] for g in range(16)], 128)
        logs = logs + more
        for g in range(16):
            inv_ref[8 * g : 8 * g + 8, :] = rows[g]
        cs = slice(128 * (k + 1), width)
        solved = dot(inv_ref[...], work_ref[rs, cs])
        for a, b in ((0, 128 * k), (128 * (k + 1), nodes)):
            if b > a:
                work_ref[a:b, cs] = work_ref[a:b, cs] - dot(work_ref[a:b, rs], solved)
        work_ref[rs, cs] = solved
    x = work_ref[:, nodes:]
    x_ref[...] = x
    grams = dot(basis, x, TN)
    loads = grams[:, :cols]
    gram = grams[:, cols:]
    rows, more = inverse([gram[8 * g : 8 * g + 8] for g in range(4)], SEG)
    odd = step % 2 == 1
    sub, lane = iotas()
    own = jnp.concatenate(rows, axis=0)
    scaled = dot(own[:, :ranks], loads)
    send_ref[:ranks, :] = jnp.where(odd, loads, scaled)
    total = jnp.sum(logs, axis=0, keepdims=True) + jnp.where(odd, 0.0, jnp.sum(more, axis=0, keepdims=True))
    chosen = jnp.where(odd, gram, own)
    slot = (step // 8) % 4
    packed = jnp.zeros((8, 128), f32)
    for q in range(4):
        packed = jnp.where(lane // SEG == (q + slot) % 4, chosen[8 * q : 8 * q + 8], packed)
    corner = (sub == 7) & (lane == SEG * ((3 + slot) % 4))
    send_ref[ranks:, :] = jnp.where(corner, jnp.broadcast_to(total[:, :1], (8, 128)), packed)


def reduce_kernel(rho_ref, recv_ref, x_ref, out_ref, ld_ref, r_ref):
    step = lax.axis_index("tm")
    rho = rho_ref[0]
    squared = rho * rho
    ranks = 32
    cols = out_ref.shape[1]
    sub, lane = iotas()
    seg = lane // SEG
    big_row = lax.broadcasted_iota(jnp.int32, (128, 128), 0) // SEG
    big_lane = lax.broadcasted_iota(jnp.int32, (128, 128), 1) // SEG
    diagonal = big_row == big_lane
    wide_lane = lax.broadcasted_iota(jnp.int32, (ranks, 128), 1) // SEG

    def blocks(packed):
        return jnp.where(diagonal, jnp.concatenate([packed] * 4, axis=0), 0.0)

    def unpack(offset):
        tiles = [recv_ref[offset + 8 * s, ranks:, :] for s in range(4)]
        top = None
        out = []
        for q in range(4):
            z = tiles[0]
            for s in range(1, 4):
                z = jnp.where(seg == (q + s) % 4, tiles[s], z)
            if q:
                z = pltpu.roll(z, 128 - SEG * q, 1)
            out.append(z)
        mirror = jnp.broadcast_to(out[0][0:1, :], (8, 128))
        mirror = pltpu.roll(mirror, 128 - 31, 1)
        out[3] = jnp.where((sub == 7) & (lane % SEG == 0), mirror, out[3])
        return jnp.concatenate(out, axis=0)

    def stack(offset):
        return jnp.concatenate([recv_ref[offset + 8 * s, :ranks, :] for s in range(4)], axis=0)

    def later(packed, by=1):
        return pltpu.roll(packed, 128 - SEG * by, 1)

    def earlier(packed, by=1):
        return pltpu.roll(packed, SEG * by, 1)

    def later_rows(v, by=1):
        return jnp.concatenate([v[SEG * by :], v[: SEG * by]], axis=0)

    def earlier_rows(v, by=1):
        return jnp.concatenate([v[-SEG * by :], v[: -SEG * by]], axis=0)

    def two(a, u, b, v):
        both = jnp.concatenate([blocks(a), blocks(b)], axis=1)
        return dot(both, jnp.concatenate([u, v], axis=0))

    def invert(packed):
        rows, logs = inverse([packed[8 * g : 8 * g + 8] for g in range(4)], SEG)
        return jnp.concatenate(rows, axis=0), logs

    odd_m = [unpack(2 * r + 1) for r in range(4)]
    odd_l = [stack(2 * r + 1) for r in range(4)]
    before_m = [jnp.where(wide_lane == 0, 0.0, earlier(odd_m[3]))] + odd_m[:3]
    before_l = [jnp.where(big_row == 0, 0.0, earlier_rows(odd_l[3]))] + odd_l[:3]
    diag = [unpack(2 * r) - squared * (odd_m[r] + before_m[r]) for r in range(4)]
    load = [stack(2 * r) + rho * (odd_l[r] + before_l[r]) for r in range(4)]
    left = [squared * m for m in before_m]
    right = [squared * m for m in odd_m]
    right[3] = jnp.where(wide_lane == 3, 0.0, right[3])

    kept = {}
    logs = jnp.zeros((8, 128), f32)
    for r in (1, 3):
        g, more = invert(diag[r])
        logs = logs + more
        p = dot(g, blocks(left[r]))
        q = dot(g, blocks(right[r]))
        c = dot(blocks(g), load[r])
        kept[r] = (p, q, c, dot(left[r], blocks(p)), dot(left[r], blocks(q)), dot(blocks(left[r]), c),
                   dot(right[r], blocks(q)), dot(right[r], blocks(p)), dot(blocks(right[r]), c))
    p1, q1, c1, lp1, lq1, lc1, rq1, rp1, rc1 = kept[1]
    p3, q3, c3, lp3, lq3, lc3, rq3, rp3, rc3 = kept[3]
    d0 = diag[0] - lp1 - earlier(rq3)
    b0 = load[0] + lc1 + earlier_rows(rc3)
    d2 = diag[2] - rq1 - lp3
    b2 = load[2] + rc1 + lc3
    l2, l2t = rp1, lq1
    r2, r2t = lq3, rp3
    g2, more = invert(d2)
    logs = logs + more
    p2 = dot(g2, blocks(l2))
    q2 = dot(g2, blocks(r2))
    c2 = dot(blocks(g2), b2)
    d0 = d0 - dot(l2t, blocks(p2)) - earlier(dot(r2t, blocks(q2)))
    b0 = b0 + dot(blocks(l2t), c2) + earlier_rows(dot(blocks(r2t), c2))
    l0 = earlier(dot(r2t, blocks(p2)))
    r0 = dot(l2t, blocks(q2))
    weight = 0.5
    for by in (1, 2):
        g0, more = invert(d0)
        logs = logs + weight * more
        p0 = dot(g0, blocks(l0))
        q0 = dot(g0, blocks(r0))
        c0 = dot(blocks(g0), b0)
        d0 = d0 - dot(l0, blocks(earlier(q0, by))) - dot(r0, blocks(later(p0, by)))
        b0 = b0 + two(l0, earlier_rows(c0, by), r0, later_rows(c0, by))
        if by == 1:
            l0, r0 = dot(l0, blocks(earlier(p0))), dot(r0, blocks(later(q0)))
        weight = weight * 0.5
    g0, more = invert(d0)
    logs = logs + 2 * weight * more
    s0 = dot(blocks(g0), b0)
    s0_next = later_rows(s0)
    s2 = c2 + two(p2, s0, q2, s0_next)
    s1 = c1 + two(p1, s0, q1, s2)
    s3 = c3 + two(p3, s2, q3, s0_next)
    even = [s0, s1, s2, s3]
    after = [s1, s2, s3, jnp.where(big_row == 3, 0.0, s0_next)]
    r_ref[0] = jnp.zeros((ranks, cols), f32)
    r_ref[33] = jnp.zeros((ranks, cols), f32)
    for r in range(4):
        o = odd_l[r] + rho * dot(blocks(odd_m[r]), even[r] + after[r])
        for s in range(4):
            r_ref[2 * r + 8 * s + 1] = even[r][SEG * s : SEG * s + SEG]
            r_ref[2 * r + 8 * s + 2] = o[SEG * s : SEG * s + SEG]
    around = rho * (r_ref[step] + r_ref[step + 2])
    out_ref[...] = x_ref[:, :cols] + dot(x_ref[:, cols : cols + ranks], around)
    total = jnp.sum(jnp.where(lane % SEG == 0, logs, 0.0))
    extra = jnp.zeros((8, 128), f32)
    for t in range(32):
        place = SEG * ((3 + t // 8) % 4)
        extra = extra + jnp.where((sub == 7) & (lane == place), recv_ref[t, ranks:, :], 0.0)
    ld_ref[0] = (total + jnp.sum(extra)) / (32.0 * out_ref.shape[0])


VMEM = pl.BlockSpec(memory_space=pltpu.VMEM)
SMEM = pl.BlockSpec(memory_space=pltpu.SMEM)


def factor(kappa, tau, near, far, modes, data):
    nodes, cols = data.shape
    parts = 2 * near.shape[0]
    return pl.pallas_call(
        factor_kernel,
        out_shape=(jax.ShapeDtypeStruct((nodes, cols + 128), f32), jax.ShapeDtypeStruct((40, 128), f32)),
        in_specs=[SMEM, SMEM, VMEM, VMEM, VMEM, VMEM],
        out_specs=(VMEM, VMEM),
        scratch_shapes=[
            pltpu.VMEM((nodes, nodes + cols + 128), f32),
            pltpu.VMEM((nodes, parts * 128), bf16),
            pltpu.VMEM((nodes, parts * 128), bf16),
            pltpu.VMEM((128, 128), f32),
        ],
        name="factor",
    )(kappa, tau, near, far, modes, data)


def reduced(rho, received, x):
    steps = received.shape[0]
    nodes, cols = x.shape[0], received.shape[2]
    return pl.pallas_call(
        reduce_kernel,
        out_shape=(jax.ShapeDtypeStruct((nodes, cols), f32), jax.ShapeDtypeStruct((1,), f32)),
        in_specs=[SMEM, VMEM, VMEM],
        out_specs=(VMEM, SMEM),
        scratch_shapes=[pltpu.VMEM((steps + 2, 32, cols), f32)],
        name="reduced",
    )(rho, received, x)


def body(prior, station_nodes, station_weights, station_counts, modes, data, kappa, tau, rho):
    parts = lax.axis_size("tile")
    steps = lax.axis_size("tm")
    band, nodes = prior.shape
    cols = data.shape[2]
    station = jnp.concatenate(
        [station_nodes[0].astype(f32).T, station_weights[0].T, station_counts.astype(f32),
         jnp.zeros((1, 128), f32)], axis=0)
    pay = jnp.concatenate([prior[:, 128 * c : 128 * (c + 1)] for c in range(nodes // 128)] + [station], axis=0)
    chips = parts // 2
    groups = [[2 * p + core for p in range(chips)] for core in range(2)]
    near = lax.all_to_all(jnp.broadcast_to(pay[None], (chips,) + pay.shape), "tile", 0, 0, axis_index_groups=groups)
    far = lax.ppermute(near, "tile", [(i, i ^ 1) for i in range(parts)])
    x, send = factor(kappa, tau, near, far, modes[0], data[0])
    received = lax.all_to_all(jnp.broadcast_to(send[None], (steps,) + send.shape), "tm", 0, 0)
    out, mean_logdet = reduced(rho, received, x)
    return (out[None, None], mean_logdet)


def solution(mesh):
    return jax.shard_map(
        body,
        mesh=mesh,
        in_specs=(
            P("tile", None),
            P("tm", "tile", None),
            P("tm", "tile", None),
            P("tm", "tile"),
            P("tm", None, None),
            P("tm", None, None),
            P("tile"),
            P("tile"),
            P("tile"),
        ),
        out_specs=(P("tm", "tile", None, None), P("tile")),
        check_vma=False,
    )
```

```python
import jax
import jax.numpy as jnp
from jax import lax
from jax.experimental import pallas as pl
from jax.experimental.pallas import tpu as pltpu
from jax.sharding import PartitionSpec as P

f32 = jnp.float32
bf16 = jnp.bfloat16
NN = ((1,), (0,))
NT = ((1,), (1,))
TN = ((0,), (0,))
SEG = 32


def dot(a, b, dims=NN, precision=lax.Precision.HIGHEST):
    return lax.dot_general(a, b, (dims, ((), ())), precision=precision, preferred_element_type=f32)


def split(v):
    high = v.astype(bf16)
    return high, (v - high.astype(f32)).astype(bf16)


def dot3(a, b, dims=NN):
    ah, al = split(a)
    bh, bl = split(b)
    left = jnp.concatenate([ah, ah, al], axis=dims[0][0])
    right = jnp.concatenate([bh, bl, bh], axis=dims[1][0])
    return lax.dot_general(left, right, (dims, ((), ())), preferred_element_type=f32)


def iotas():
    return (
        lax.broadcasted_iota(jnp.int32, (8, 128), 0),
        lax.broadcasted_iota(jnp.int32, (8, 128), 1),
    )


def row_of(v, k):
    return jnp.broadcast_to(v[k : k + 1, :], v.shape)


def eliminate(columns, panel):
    sub, _ = iotas()
    own = list(columns)
    dets = jnp.ones((8, 128), f32)
    for k in range(0, 8, 2):
        ca, cb = own[k], own[k + 1]
        paa, pab, pbb = row_of(ca, k), row_of(cb, k), row_of(cb, k + 1)
        det = paa * pbb - pab * pab
        inv = 1.0 / det
        on_a, on_b = sub == k, sub == k + 1
        both = on_a | on_b
        na = jnp.where(on_a, -pbb, jnp.where(on_b, pab, ca * pbb - cb * pab))
        nb = jnp.where(on_a, pab, jnp.where(on_b, -paa, cb * paa - ca * pab))
        dets = jnp.where(on_a, det, dets)

        def step(v):
            return jnp.where(both, 0.0, v) - (na * row_of(v, k) + nb * row_of(v, k + 1)) * inv

        own[k + 2 :] = [step(v) for v in own[k + 2 :]]
        panel = step(panel)
    return panel, dets


def downdate(columns, spread):
    t = [columns[k] * spread[k] for k in range(8)]
    return ((t[0] + t[1]) + (t[2] + t[3])) + ((t[4] + t[5]) + (t[6] + t[7]))


def inverse128(rows):
    sub, lane = iotas()
    rows = list(rows)
    logs = jnp.zeros((8, 128), f32)
    lower, scaled = [], []
    for b in range(16):
        start = 8 * b
        before = lane < start
        until = lane < start + 8
        pivots = until & jnp.logical_not(before)
        identity = jnp.where(lane - start == sub, 1.0, 0.0)
        columns = [[jnp.broadcast_to(rows[g][:, start + k : start + k + 1], (8, 128)) for k in range(8)]
                   for g in range(b, 16)]
        panel, dets = eliminate(columns[0], jnp.where(pivots, identity, rows[b]))
        logs = logs + jnp.log(dets)
        lower.append(jnp.where(before, rows[b], identity))
        scaled.append(jnp.where(until, panel, 0.0))
        spread = [row_of(panel, k) for k in range(8)]
        for g in range(b + 1, 16):
            rows[g] = jnp.where(pivots, 0.0, rows[g]) - downdate(columns[g - b], spread)
    return dot3(jnp.concatenate(lower, axis=0), jnp.concatenate(scaled, axis=0), TN), logs


def inverse32(rows):
    sub, lane = iotas()
    local = lane % SEG
    first = lane - local
    logs = jnp.zeros((8, 128), f32)
    rows = list(rows)
    for b in range(4):
        start = 8 * b
        pivots = (local >= start) & (local < start + 8)
        columns = [[jnp.take_along_axis(rows[g], first + (start + k), axis=1) for k in range(8)] for g in range(4)]
        panel, dets = eliminate(columns[b], jnp.where(pivots, jnp.where(local - start == sub, 1.0, 0.0), rows[b]))
        logs = logs + jnp.log(dets)
        spread = [row_of(panel, k) for k in range(8)]
        for g in range(4):
            if g != b:
                rows[g] = jnp.where(pivots, 0.0, rows[g]) - downdate(columns[g], spread)
        rows[b] = panel
    return rows, logs


def factor_kernel(kappa_ref, tau_ref, near_ref, far_ref, modes_ref, data_ref, x_ref, send_ref,
                  work_ref, high_ref, low_ref):
    step = lax.axis_index("tm")
    ranks, nodes = modes_ref.shape
    cols = data_ref.shape[1]
    chips = near_ref.shape[0]
    parts = 2 * chips
    core = lax.axis_index("tile") % 2
    band = nodes // parts
    tiles = nodes // 128
    kappa = kappa_ref[0]
    tau = tau_ref[0]
    ids = lax.broadcasted_iota(jnp.int32, (nodes, 128), 0).astype(f32)
    for p in range(parts):
        s = (near_ref if p < chips else far_ref)[p % chips, tiles * band :, :]
        n0, n1, n2, w0, w1, w2 = [s[i : i + 1] for i in range(6)]
        root = jnp.sqrt(s[6:7])
        same01 = n1 == n0
        same02 = n2 == n0
        same12 = (n2 == n1) & jnp.logical_not(same02)
        w0 = w0 + jnp.where(same01, w1, 0.0) + jnp.where(same02, w2, 0.0)
        w1 = w1 + jnp.where(same12, w2, 0.0)
        w0, w1, w2 = w0 * root, w1 * root, w2 * root
        h0, h1, h2 = [w.astype(bf16).astype(f32) for w in (w0, w1, w2)]
        m0, m1, m2 = ids == n0, ids == n1, ids == n2

        def place(a, b, c):
            return jnp.where(m0, a, jnp.where(m1, b, jnp.where(m2, c, 0.0))).astype(bf16)

        at = slice(p * 128, (p + 1) * 128)
        high_ref[:, at] = place(h0, h1, h2)
        low_ref[:, at] = place(w0 - h0, w1 - h1, w2 - h2)
    half = nodes // 2
    for i in range(2):
        rs = slice(i * half, (i + 1) * half)
        high = high_ref[rs, :]
        gram = (dot(high, high_ref[...], NT, None) + dot(high, low_ref[...], NT, None)
                + dot(low_ref[rs, :], high_ref[...], NT, None))
        work_ref[rs, :nodes] = tau * gram
    for ref, side in ((near_ref, core), (far_ref, 1 - core)):
        for p in range(chips):
            at = pl.ds(pl.multiple_of((2 * p + side) * band, band), band)
            for c in range(tiles):
                cs = slice(c * 128, (c + 1) * 128)
                work_ref[at, cs] = work_ref[at, cs] + kappa * ref[p, c * band : (c + 1) * band, :]
    work_ref[:, nodes : nodes + cols] = data_ref[...]
    basis = modes_ref[...]
    four = jnp.concatenate([basis] * (128 // ranks), axis=0)
    for c in range(tiles):
        rs = slice(128 * c, 128 * (c + 1))
        work_ref[rs, nodes + cols :] = four[:, rs].T
    width = nodes + cols + 128
    logs = jnp.zeros((8, 128), f32)
    for k in range(tiles):
        rs = slice(128 * k, 128 * (k + 1))
        inv, more = inverse128([work_ref[128 * k + 8 * g : 128 * k + 8 * g + 8, rs] for g in range(16)])
        logs = logs + more
        cs = slice(128 * (k + 1), width)
        solved = dot3(inv, work_ref[rs, cs])
        for a, b in ((0, 128 * k), (128 * (k + 1), nodes)):
            if b > a:
                work_ref[a:b, cs] = work_ref[a:b, cs] - dot3(work_ref[a:b, rs], solved)
        work_ref[rs, cs] = solved
    x = work_ref[:, nodes:]
    x_ref[...] = x
    grams = dot(basis, x)
    loads = grams[:, :cols]
    gram = grams[:, cols:]
    rows, more = inverse32([gram[8 * g : 8 * g + 8] for g in range(4)])
    odd = step % 2 == 1
    sub, lane = iotas()
    own = jnp.concatenate(rows, axis=0)
    scaled = dot(own[:, :ranks], loads)
    top = jnp.where(odd, loads, scaled)
    total = jnp.sum(logs, axis=0, keepdims=True) + jnp.where(odd, 0.0, jnp.sum(more, axis=0, keepdims=True))
    chosen = jnp.where(odd, gram, own)
    slot = (step // 8) % 4
    packed = jnp.zeros((8, 128), f32)
    for q in range(4):
        packed = jnp.where(lane // SEG == (q + slot) % 4, chosen[8 * q : 8 * q + 8], packed)
    corner = (sub == 7) & (lane == SEG * ((3 + slot) % 4))
    bottom = jnp.where(corner, jnp.broadcast_to(total[:, :1], (8, 128)), packed)
    send_ref[:, :ranks, :] = jnp.broadcast_to(top[None], (send_ref.shape[0],) + top.shape)
    send_ref[:, ranks:, :] = jnp.broadcast_to(bottom[None], (send_ref.shape[0],) + bottom.shape)


def reduce_kernel(rho_ref, recv_ref, x_ref, out_ref, ld_ref, r_ref):
    step = lax.axis_index("tm")
    rho = rho_ref[0]
    squared = rho * rho
    ranks = 32
    cols = out_ref.shape[1]
    sub, lane = iotas()
    seg = lane // SEG
    big_row = lax.broadcasted_iota(jnp.int32, (128, 128), 0) // SEG
    big_lane = lax.broadcasted_iota(jnp.int32, (128, 128), 1) // SEG
    diagonal = big_row == big_lane
    wide_lane = lax.broadcasted_iota(jnp.int32, (ranks, 128), 1) // SEG

    def blocks(packed):
        return jnp.where(diagonal, jnp.concatenate([packed] * 4, axis=0), 0.0)

    def unpack(offset):
        tiles = [recv_ref[offset + 8 * s, ranks:, :] for s in range(4)]
        top = None
        out = []
        for q in range(4):
            z = tiles[0]
            for s in range(1, 4):
                z = jnp.where(seg == (q + s) % 4, tiles[s], z)
            if q:
                z = pltpu.roll(z, 128 - SEG * q, 1)
            out.append(z)
        mirror = jnp.broadcast_to(out[0][0:1, :], (8, 128))
        mirror = pltpu.roll(mirror, 128 - 31, 1)
        out[3] = jnp.where((sub == 7) & (lane % SEG == 0), mirror, out[3])
        return jnp.concatenate(out, axis=0)

    def stack(offset):
        return jnp.concatenate([recv_ref[offset + 8 * s, :ranks, :] for s in range(4)], axis=0)

    def later(packed, by=1):
        return pltpu.roll(packed, 128 - SEG * by, 1)

    def earlier(packed, by=1):
        return pltpu.roll(packed, SEG * by, 1)

    def later_rows(v, by=1):
        return jnp.concatenate([v[SEG * by :], v[: SEG * by]], axis=0)

    def earlier_rows(v, by=1):
        return jnp.concatenate([v[-SEG * by :], v[: -SEG * by]], axis=0)

    def two(a, u, b, v):
        both = jnp.concatenate([blocks(a), blocks(b)], axis=1)
        return dot(both, jnp.concatenate([u, v], axis=0))

    def invert(packed):
        rows, logs = inverse32([packed[8 * g : 8 * g + 8] for g in range(4)])
        return jnp.concatenate(rows, axis=0), logs

    odd_m = [unpack(2 * r + 1) for r in range(4)]
    odd_l = [stack(2 * r + 1) for r in range(4)]
    before_m = [jnp.where(wide_lane == 0, 0.0, earlier(odd_m[3]))] + odd_m[:3]
    before_l = [jnp.where(big_row == 0, 0.0, earlier_rows(odd_l[3]))] + odd_l[:3]
    diag = [unpack(2 * r) - squared * (odd_m[r] + before_m[r]) for r in range(4)]
    load = [stack(2 * r) + rho * (odd_l[r] + before_l[r]) for r in range(4)]
    left = [squared * m for m in before_m]
    right = [squared * m for m in odd_m]
    right[3] = jnp.where(wide_lane == 3, 0.0, right[3])

    kept = {}
    logs = jnp.zeros((8, 128), f32)
    for r in (1, 3):
        g, more = invert(diag[r])
        logs = logs + more
        p = dot(g, blocks(left[r]))
        q = dot(g, blocks(right[r]))
        c = dot(blocks(g), load[r])
        kept[r] = (p, q, c, dot(left[r], blocks(p)), dot(left[r], blocks(q)), dot(blocks(left[r]), c),
                   dot(right[r], blocks(q)), dot(right[r], blocks(p)), dot(blocks(right[r]), c))
    p1, q1, c1, lp1, lq1, lc1, rq1, rp1, rc1 = kept[1]
    p3, q3, c3, lp3, lq3, lc3, rq3, rp3, rc3 = kept[3]
    d0 = diag[0] - lp1 - earlier(rq3)
    b0 = load[0] + lc1 + earlier_rows(rc3)
    d2 = diag[2] - rq1 - lp3
    b2 = load[2] + rc1 + lc3
    l2, l2t = rp1, lq1
    r2, r2t = lq3, rp3
    g2, more = invert(d2)
    logs = logs + more
    p2 = dot(g2, blocks(l2))
    q2 = dot(g2, blocks(r2))
    c2 = dot(blocks(g2), b2)
    d0 = d0 - dot(l2t, blocks(p2)) - earlier(dot(r2t, blocks(q2)))
    b0 = b0 + dot(blocks(l2t), c2) + earlier_rows(dot(blocks(r2t), c2))
    l0 = earlier(dot(r2t, blocks(p2)))
    r0 = dot(l2t, blocks(q2))
    weight = 0.5
    for by in (1, 2):
        g0, more = invert(d0)
        logs = logs + weight * more
        p0 = dot(g0, blocks(l0))
        q0 = dot(g0, blocks(r0))
        c0 = dot(blocks(g0), b0)
        d0 = d0 - dot(l0, blocks(earlier(q0, by))) - dot(r0, blocks(later(p0, by)))
        b0 = b0 + two(l0, earlier_rows(c0, by), r0, later_rows(c0, by))
        if by == 1:
            l0, r0 = dot(l0, blocks(earlier(p0))), dot(r0, blocks(later(q0)))
        weight = weight * 0.5
    g0, more = invert(d0)
    logs = logs + 2 * weight * more
    s0 = dot(blocks(g0), b0)
    s0_next = later_rows(s0)
    s2 = c2 + two(p2, s0, q2, s0_next)
    s1 = c1 + two(p1, s0, q1, s2)
    s3 = c3 + two(p3, s2, q3, s0_next)
    even = [s0, s1, s2, s3]
    after = [s1, s2, s3, jnp.where(big_row == 3, 0.0, s0_next)]
    r_ref[0] = jnp.zeros((ranks, cols), f32)
    r_ref[33] = jnp.zeros((ranks, cols), f32)
    for r in range(4):
        o = odd_l[r] + rho * dot(blocks(odd_m[r]), even[r] + after[r])
        for s in range(4):
            r_ref[2 * r + 8 * s + 1] = even[r][SEG * s : SEG * s + SEG]
            r_ref[2 * r + 8 * s + 2] = o[SEG * s : SEG * s + SEG]
    around = rho * (r_ref[step] + r_ref[step + 2])
    out_ref[...] = x_ref[:, :cols] + dot(x_ref[:, cols : cols + ranks], around)
    total = jnp.sum(jnp.where(lane % SEG == 0, logs, 0.0))
    extra = jnp.zeros((8, 128), f32)
    for t in range(32):
        place = SEG * ((3 + t // 8) % 4)
        extra = extra + jnp.where((sub == 7) & (lane == place), recv_ref[t, ranks:, :], 0.0)
    ld_ref[0] = (total + jnp.sum(extra)) / (32.0 * out_ref.shape[0])


VMEM = pl.BlockSpec(memory_space=pltpu.VMEM)
SMEM = pl.BlockSpec(memory_space=pltpu.SMEM)


def factor(kappa, tau, near, far, modes, data, steps):
    nodes, cols = data.shape
    parts = 2 * near.shape[0]
    return pl.pallas_call(
        factor_kernel,
        out_shape=(jax.ShapeDtypeStruct((nodes, cols + 128), f32), jax.ShapeDtypeStruct((steps, 40, 128), f32)),
        in_specs=[SMEM, SMEM, VMEM, VMEM, VMEM, VMEM],
        out_specs=(VMEM, VMEM),
        scratch_shapes=[
            pltpu.VMEM((nodes, nodes + cols + 128), f32),
            pltpu.VMEM((nodes, parts * 128), bf16),
            pltpu.VMEM((nodes, parts * 128), bf16),
        ],
        name="factor",
    )(kappa, tau, near, far, modes, data)


def reduced(rho, received, x):
    steps = received.shape[0]
    nodes, cols = x.shape[0], received.shape[2]
    return pl.pallas_call(
        reduce_kernel,
        out_shape=(jax.ShapeDtypeStruct((nodes, cols), f32), jax.ShapeDtypeStruct((1,), f32)),
        in_specs=[SMEM, VMEM, VMEM],
        out_specs=(VMEM, SMEM),
        scratch_shapes=[pltpu.VMEM((steps + 2, 32, cols), f32)],
        name="reduced",
    )(rho, received, x)


def body(prior, station_nodes, station_weights, station_counts, modes, data, kappa, tau, rho):
    parts = lax.axis_size("tile")
    steps = lax.axis_size("tm")
    band, nodes = prior.shape
    cols = data.shape[2]
    station = jnp.concatenate(
        [station_nodes[0].astype(f32).T, station_weights[0].T, station_counts.astype(f32),
         jnp.zeros((1, 128), f32)], axis=0)
    pay = jnp.concatenate([prior[:, 128 * c : 128 * (c + 1)] for c in range(nodes // 128)] + [station], axis=0)
    chips = parts // 2
    groups = [[2 * p + core for p in range(chips)] for core in range(2)]
    near = lax.all_to_all(jnp.broadcast_to(pay[None], (chips,) + pay.shape), "tile", 0, 0, axis_index_groups=groups)
    far = lax.ppermute(near, "tile", [(i, i ^ 1) for i in range(parts)])
    x, send = factor(kappa, tau, near, far, modes[0].T, data[0], steps)
    received = lax.all_to_all(send, "tm", 0, 0)
    out, mean_logdet = reduced(rho, received, x)
    return (out[None, None], mean_logdet)


def solution(mesh):
    return jax.shard_map(
        body,
        mesh=mesh,
        in_specs=(
            P("tile", None),
            P("tm", "tile", None),
            P("tm", "tile", None),
            P("tm", "tile"),
            P("tm", None, None),
            P("tm", None, None),
            P("tile"),
            P("tile"),
            P("tile"),
        ),
        out_specs=(P("tm", "tile", None, None), P("tile")),
        check_vma=False,
    )
```

```python
import jax
import jax.numpy as jnp
from jax import lax
from jax.experimental import pallas as pl
from jax.experimental.pallas import tpu as pltpu
from jax.sharding import PartitionSpec as P

f32 = jnp.float32
bf16 = jnp.bfloat16
NN = ((1,), (0,))
NT = ((1,), (1,))
TN = ((0,), (0,))
SEG = 32


def dot(a, b, dims=NN, precision=lax.Precision.HIGHEST):
    return lax.dot_general(a, b, (dims, ((), ())), precision=precision, preferred_element_type=f32)


def split(v):
    high = v.astype(bf16)
    return high, (v - high.astype(f32)).astype(bf16)


def dot3(a, b, dims=NN):
    ah, al = split(a)
    bh, bl = split(b)
    left = jnp.concatenate([ah, ah, al], axis=dims[0][0])
    right = jnp.concatenate([bh, bl, bh], axis=dims[1][0])
    return lax.dot_general(left, right, (dims, ((), ())), preferred_element_type=f32)


def iotas():
    return (
        lax.broadcasted_iota(jnp.int32, (8, 128), 0),
        lax.broadcasted_iota(jnp.int32, (8, 128), 1),
    )


def row_of(v, k):
    return jnp.broadcast_to(v[k : k + 1, :], v.shape)


def eliminate(columns, panel):
    sub, _ = iotas()
    own = list(columns)
    dets = jnp.ones((8, 128), f32)
    for k in range(0, 8, 2):
        ca, cb = own[k], own[k + 1]
        paa, pab, pbb = row_of(ca, k), row_of(cb, k), row_of(cb, k + 1)
        det = paa * pbb - pab * pab
        inv = 1.0 / det
        on_a, on_b = sub == k, sub == k + 1
        both = on_a | on_b
        na = jnp.where(on_a, -pbb, jnp.where(on_b, pab, ca * pbb - cb * pab))
        nb = jnp.where(on_a, pab, jnp.where(on_b, -paa, cb * paa - ca * pab))
        dets = jnp.where(on_a, det, dets)

        def step(v):
            return jnp.where(both, 0.0, v) - (na * row_of(v, k) + nb * row_of(v, k + 1)) * inv

        own[k + 2 :] = [step(v) for v in own[k + 2 :]]
        panel = step(panel)
    return panel, dets


def downdate(columns, spread):
    t = [columns[k] * spread[k] for k in range(8)]
    return ((t[0] + t[1]) + (t[2] + t[3])) + ((t[4] + t[5]) + (t[6] + t[7]))


def inverse128(rows):
    sub, lane = iotas()
    rows = list(rows)
    logs = jnp.zeros((8, 128), f32)
    lower, scaled = [], []
    for b in range(16):
        start = 8 * b
        before = lane < start
        until = lane < start + 8
        pivots = until & jnp.logical_not(before)
        identity = jnp.where(lane - start == sub, 1.0, 0.0)
        columns = [[jnp.broadcast_to(rows[g][:, start + k : start + k + 1], (8, 128)) for k in range(8)]
                   for g in range(b, 16)]
        panel, dets = eliminate(columns[0], jnp.where(pivots, identity, rows[b]))
        logs = logs + jnp.log(dets)
        lower.append(jnp.where(before, rows[b], identity))
        scaled.append(jnp.where(until, panel, 0.0))
        spread = [row_of(panel, k) for k in range(8)]
        for g in range(b + 1, 16):
            rows[g] = jnp.where(pivots, 0.0, rows[g]) - downdate(columns[g - b], spread)
    return dot3(jnp.concatenate(lower, axis=0), jnp.concatenate(scaled, axis=0), TN), logs


def inverse32(rows):
    sub, lane = iotas()
    local = lane % SEG
    first = lane - local
    logs = jnp.zeros((8, 128), f32)
    rows = list(rows)
    for b in range(4):
        start = 8 * b
        pivots = (local >= start) & (local < start + 8)
        columns = [[jnp.take_along_axis(rows[g], first + (start + k), axis=1) for k in range(8)] for g in range(4)]
        panel, dets = eliminate(columns[b], jnp.where(pivots, jnp.where(local - start == sub, 1.0, 0.0), rows[b]))
        logs = logs + jnp.log(dets)
        spread = [row_of(panel, k) for k in range(8)]
        for g in range(4):
            if g != b:
                rows[g] = jnp.where(pivots, 0.0, rows[g]) - downdate(columns[g], spread)
        rows[b] = panel
    return rows, logs


def assemble(kappa, core, near_ref, far_ref, work_ref, strip_ref):
    chips = near_ref.shape[0]
    nodes = work_ref.shape[0]
    lane = lax.broadcasted_iota(jnp.int32, (32, 128), 1)
    tiles = nodes // 128
    for i in range(2 * chips):
        own = (core == 0) if i % 2 == 0 else (core == 1)
        part = kappa * jnp.where(own, near_ref[i // 2, :72, :], far_ref[i // 2, :72, :])
        shift = SEG * (i % 4)
        last = part[64:72]
        eighth = jnp.concatenate(
            [last if q == 0 else pltpu.roll(last, 128 - SEG * q, 1) for q in range(4)], axis=0)
        blocks = [part[:32], part[32:64], jnp.where(lane < SEG, eighth, 0.0)]
        bare = [jnp.where(lane < SEG, 0.0, part[:32]), part[32:64]]
        if shift:
            blocks = [pltpu.roll(v, shift, 1) for v in blocks]
            bare = [pltpu.roll(v, shift, 1) for v in bare]
        zero = jnp.zeros((32, 128), f32)
        rows = slice(32 * i, 32 * i + 32)

        def laid(pieces, ref):
            pieces = pieces + [zero] * (tiles - len(pieces))
            for c in range(tiles):
                at = (i // 4 + c) % tiles
                v = jnp.where(lane < shift, pieces[c - 1], pieces[c]) if shift else pieces[c]
                ref[rows, 128 * at : 128 * at + 128] = v

        laid(blocks, work_ref)
        laid(bare, strip_ref)
    for a in range(tiles):
        for off in range(3):
            b = (a + off) % tiles
            ra, rb = slice(128 * a, 128 * a + 128), slice(128 * b, 128 * b + 128)
            work_ref[rb, ra] = work_ref[rb, ra] + strip_ref[ra, rb].T


def factor_kernel(kappa_ref, tau_ref, near_ref, far_ref, modes_ref, data_ref, x_ref, send_ref,
                  work_ref, high_ref, low_ref, strip_ref):
    step = lax.axis_index("tm")
    ranks, nodes = modes_ref.shape
    cols = data_ref.shape[1]
    chips = near_ref.shape[0]
    parts = 2 * chips
    core = lax.axis_index("tile") % 2
    band = nodes // parts
    tiles = nodes // 128
    kappa = kappa_ref[0]
    tau = tau_ref[0]
    ids = lax.broadcasted_iota(jnp.int32, (nodes, 128), 0).astype(f32)
    for p in range(parts):
        s = (near_ref if p < chips else far_ref)[p % chips, 72:, :]
        n0, n1, n2, w0, w1, w2 = [s[i : i + 1] for i in range(6)]
        root = jnp.sqrt(s[6:7])
        same01 = n1 == n0
        same02 = n2 == n0
        same12 = (n2 == n1) & jnp.logical_not(same02)
        w0 = w0 + jnp.where(same01, w1, 0.0) + jnp.where(same02, w2, 0.0)
        w1 = w1 + jnp.where(same12, w2, 0.0)
        w0, w1, w2 = w0 * root, w1 * root, w2 * root
        h0, h1, h2 = [w.astype(bf16).astype(f32) for w in (w0, w1, w2)]
        m0, m1, m2 = ids == n0, ids == n1, ids == n2

        def place(a, b, c):
            return jnp.where(m0, a, jnp.where(m1, b, jnp.where(m2, c, 0.0))).astype(bf16)

        at = slice(p * 128, (p + 1) * 128)
        high_ref[:, at] = place(h0, h1, h2)
        low_ref[:, at] = place(w0 - h0, w1 - h1, w2 - h2)
    assemble(kappa, core, near_ref, far_ref, work_ref, strip_ref)
    half = nodes // 2
    for i in range(2):
        rs = slice(i * half, (i + 1) * half)
        high = high_ref[rs, :]
        gram = (dot(high, high_ref[...], NT, None) + dot(high, low_ref[...], NT, None)
                + dot(low_ref[rs, :], high_ref[...], NT, None))
        work_ref[rs, :nodes] = work_ref[rs, :nodes] + tau * gram
    work_ref[:, nodes : nodes + cols] = data_ref[...]
    basis = modes_ref[...]
    four = jnp.concatenate([basis] * (128 // ranks), axis=0)
    for c in range(tiles):
        rs = slice(128 * c, 128 * (c + 1))
        work_ref[rs, nodes + cols :] = four[:, rs].T
    width = nodes + cols + 128
    logs = jnp.zeros((8, 128), f32)
    for k in range(tiles):
        rs = slice(128 * k, 128 * (k + 1))
        inv, more = inverse128([work_ref[128 * k + 8 * g : 128 * k + 8 * g + 8, rs] for g in range(16)])
        logs = logs + more
        cs = slice(128 * (k + 1), width)
        solved = dot3(inv, work_ref[rs, cs])
        for a, b in ((0, 128 * k), (128 * (k + 1), nodes)):
            if b > a:
                work_ref[a:b, cs] = work_ref[a:b, cs] - dot3(work_ref[a:b, rs], solved)
        work_ref[rs, cs] = solved
    x = work_ref[:, nodes:]
    x_ref[...] = x
    grams = dot(basis, x)
    loads = grams[:, :cols]
    gram = grams[:, cols:]
    rows, more = inverse32([gram[8 * g : 8 * g + 8] for g in range(4)])
    odd = step % 2 == 1
    sub, lane = iotas()
    own = jnp.concatenate(rows, axis=0)
    scaled = dot(own[:, :ranks], loads)
    top = jnp.where(odd, loads, scaled)
    total = jnp.sum(logs, axis=0, keepdims=True) + jnp.where(odd, 0.0, jnp.sum(more, axis=0, keepdims=True))
    chosen = jnp.where(odd, gram, own)
    slot = (step // 8) % 4
    packed = jnp.zeros((8, 128), f32)
    for q in range(4):
        packed = jnp.where(lane // SEG == (q + slot) % 4, chosen[8 * q : 8 * q + 8], packed)
    corner = (sub == 7) & (lane == SEG * ((3 + slot) % 4))
    bottom = jnp.where(corner, jnp.broadcast_to(total[:, :1], (8, 128)), packed)
    send_ref[:, :ranks, :] = jnp.broadcast_to(top[None], (send_ref.shape[0],) + top.shape)
    send_ref[:, ranks:, :] = jnp.broadcast_to(bottom[None], (send_ref.shape[0],) + bottom.shape)


def reduce_kernel(rho_ref, recv_ref, x_ref, out_ref, ld_ref, r_ref):
    step = lax.axis_index("tm")
    rho = rho_ref[0]
    squared = rho * rho
    ranks = 32
    cols = out_ref.shape[1]
    sub, lane = iotas()
    seg = lane // SEG
    big_row = lax.broadcasted_iota(jnp.int32, (128, 128), 0) // SEG
    big_lane = lax.broadcasted_iota(jnp.int32, (128, 128), 1) // SEG
    diagonal = big_row == big_lane
    wide_lane = lax.broadcasted_iota(jnp.int32, (ranks, 128), 1) // SEG

    def blocks(packed):
        return jnp.where(diagonal, jnp.concatenate([packed] * 4, axis=0), 0.0)

    def unpack(offset):
        tiles = [recv_ref[offset + 8 * s, ranks:, :] for s in range(4)]
        top = None
        out = []
        for q in range(4):
            z = tiles[0]
            for s in range(1, 4):
                z = jnp.where(seg == (q + s) % 4, tiles[s], z)
            if q:
                z = pltpu.roll(z, 128 - SEG * q, 1)
            out.append(z)
        mirror = jnp.broadcast_to(out[0][0:1, :], (8, 128))
        mirror = pltpu.roll(mirror, 128 - 31, 1)
        out[3] = jnp.where((sub == 7) & (lane % SEG == 0), mirror, out[3])
        return jnp.concatenate(out, axis=0)

    def stack(offset):
        return jnp.concatenate([recv_ref[offset + 8 * s, :ranks, :] for s in range(4)], axis=0)

    def later(packed, by=1):
        return pltpu.roll(packed, 128 - SEG * by, 1)

    def earlier(packed, by=1):
        return pltpu.roll(packed, SEG * by, 1)

    def later_rows(v, by=1):
        return jnp.concatenate([v[SEG * by :], v[: SEG * by]], axis=0)

    def earlier_rows(v, by=1):
        return jnp.concatenate([v[-SEG * by :], v[: -SEG * by]], axis=0)

    def two(a, u, b, v):
        both = jnp.concatenate([blocks(a), blocks(b)], axis=1)
        return dot(both, jnp.concatenate([u, v], axis=0))

    def invert(packed):
        rows, logs = inverse32([packed[8 * g : 8 * g + 8] for g in range(4)])
        return jnp.concatenate(rows, axis=0), logs

    odd_m = [unpack(2 * r + 1) for r in range(4)]
    odd_l = [stack(2 * r + 1) for r in range(4)]
    before_m = [jnp.where(wide_lane == 0, 0.0, earlier(odd_m[3]))] + odd_m[:3]
    before_l = [jnp.where(big_row == 0, 0.0, earlier_rows(odd_l[3]))] + odd_l[:3]
    diag = [unpack(2 * r) - squared * (odd_m[r] + before_m[r]) for r in range(4)]
    load = [stack(2 * r) + rho * (odd_l[r] + before_l[r]) for r in range(4)]
    left = [squared * m for m in before_m]
    right = [squared * m for m in odd_m]
    right[3] = jnp.where(wide_lane == 3, 0.0, right[3])

    kept = {}
    logs = jnp.zeros((8, 128), f32)
    for r in (1, 3):
        g, more = invert(diag[r])
        logs = logs + more
        p = dot(g, blocks(left[r]))
        q = dot(g, blocks(right[r]))
        c = dot(blocks(g), load[r])
        kept[r] = (p, q, c, dot(left[r], blocks(p)), dot(left[r], blocks(q)), dot(blocks(left[r]), c),
                   dot(right[r], blocks(q)), dot(right[r], blocks(p)), dot(blocks(right[r]), c))
    p1, q1, c1, lp1, lq1, lc1, rq1, rp1, rc1 = kept[1]
    p3, q3, c3, lp3, lq3, lc3, rq3, rp3, rc3 = kept[3]
    d0 = diag[0] - lp1 - earlier(rq3)
    b0 = load[0] + lc1 + earlier_rows(rc3)
    d2 = diag[2] - rq1 - lp3
    b2 = load[2] + rc1 + lc3
    l2, l2t = rp1, lq1
    r2, r2t = lq3, rp3
    g2, more = invert(d2)
    logs = logs + more
    p2 = dot(g2, blocks(l2))
    q2 = dot(g2, blocks(r2))
    c2 = dot(blocks(g2), b2)
    d0 = d0 - dot(l2t, blocks(p2)) - earlier(dot(r2t, blocks(q2)))
    b0 = b0 + dot(blocks(l2t), c2) + earlier_rows(dot(blocks(r2t), c2))
    l0 = earlier(dot(r2t, blocks(p2)))
    r0 = dot(l2t, blocks(q2))
    weight = 0.5
    for by in (1, 2):
        g0, more = invert(d0)
        logs = logs + weight * more
        p0 = dot(g0, blocks(l0))
        q0 = dot(g0, blocks(r0))
        c0 = dot(blocks(g0), b0)
        d0 = d0 - dot(l0, blocks(earlier(q0, by))) - dot(r0, blocks(later(p0, by)))
        b0 = b0 + two(l0, earlier_rows(c0, by), r0, later_rows(c0, by))
        if by == 1:
            l0, r0 = dot(l0, blocks(earlier(p0))), dot(r0, blocks(later(q0)))
        weight = weight * 0.5
    g0, more = invert(d0)
    logs = logs + 2 * weight * more
    s0 = dot(blocks(g0), b0)
    s0_next = later_rows(s0)
    s2 = c2 + two(p2, s0, q2, s0_next)
    s1 = c1 + two(p1, s0, q1, s2)
    s3 = c3 + two(p3, s2, q3, s0_next)
    even = [s0, s1, s2, s3]
    after = [s1, s2, s3, jnp.where(big_row == 3, 0.0, s0_next)]
    r_ref[0] = jnp.zeros((ranks, cols), f32)
    r_ref[33] = jnp.zeros((ranks, cols), f32)
    for r in range(4):
        o = odd_l[r] + rho * dot(blocks(odd_m[r]), even[r] + after[r])
        for s in range(4):
            r_ref[2 * r + 8 * s + 1] = even[r][SEG * s : SEG * s + SEG]
            r_ref[2 * r + 8 * s + 2] = o[SEG * s : SEG * s + SEG]
    around = rho * (r_ref[step] + r_ref[step + 2])
    out_ref[...] = x_ref[:, :cols] + dot(x_ref[:, cols : cols + ranks], around)
    total = jnp.sum(jnp.where(lane % SEG == 0, logs, 0.0))
    extra = jnp.zeros((8, 128), f32)
    for t in range(32):
        place = SEG * ((3 + t // 8) % 4)
        extra = extra + jnp.where((sub == 7) & (lane == place), recv_ref[t, ranks:, :], 0.0)
    ld_ref[0] = (total + jnp.sum(extra)) / (32.0 * out_ref.shape[0])


VMEM = pl.BlockSpec(memory_space=pltpu.VMEM)
SMEM = pl.BlockSpec(memory_space=pltpu.SMEM)


def pack_kernel(prior_ref, station_ref, out_ref):
    i = lax.axis_index("tile")
    nodes = prior_ref.shape[1]
    chips = out_ref.shape[0]
    _, lane = iotas()
    rolled = pltpu.roll(prior_ref[...], (nodes - SEG * i) % nodes, 1)
    far = rolled[:, 256:384]
    eighth = jnp.zeros((8, 128), f32)
    for q in range(4):
        v = far[8 * q : 8 * q + 8]
        eighth = jnp.where(lane // SEG == q, v if q == 0 else pltpu.roll(v, SEG * q, 1), eighth)
    whole = jnp.concatenate([rolled[:, :128], rolled[:, 128:256], eighth, station_ref[...]], axis=0)
    out_ref[...] = jnp.broadcast_to(whole[None], (chips,) + whole.shape)


def packed(prior, station, chips):
    return pl.pallas_call(
        pack_kernel,
        out_shape=jax.ShapeDtypeStruct((chips, 80, 128), f32),
        in_specs=[VMEM, VMEM],
        out_specs=VMEM,
        name="pack",
    )(prior, station)


def factor(kappa, tau, near, far, modes, data, steps):
    nodes, cols = data.shape
    parts = 2 * near.shape[0]
    return pl.pallas_call(
        factor_kernel,
        out_shape=(jax.ShapeDtypeStruct((nodes, cols + 128), f32), jax.ShapeDtypeStruct((steps, 40, 128), f32)),
        in_specs=[SMEM, SMEM, VMEM, VMEM, VMEM, VMEM],
        out_specs=(VMEM, VMEM),
        scratch_shapes=[
            pltpu.VMEM((nodes, nodes + cols + 128), f32),
            pltpu.VMEM((nodes, parts * 128), bf16),
            pltpu.VMEM((nodes, parts * 128), bf16),
            pltpu.VMEM((nodes, nodes), f32),
        ],
        name="factor",
    )(kappa, tau, near, far, modes, data)


def reduced(rho, received, x):
    steps = received.shape[0]
    nodes, cols = x.shape[0], received.shape[2]
    return pl.pallas_call(
        reduce_kernel,
        out_shape=(jax.ShapeDtypeStruct((nodes, cols), f32), jax.ShapeDtypeStruct((1,), f32)),
        in_specs=[SMEM, VMEM, VMEM],
        out_specs=(VMEM, SMEM),
        scratch_shapes=[pltpu.VMEM((steps + 2, 32, cols), f32)],
        name="reduced",
    )(rho, received, x)


def body(prior, station_nodes, station_weights, station_counts, modes, data, kappa, tau, rho):
    parts = lax.axis_size("tile")
    steps = lax.axis_size("tm")
    band, nodes = prior.shape
    cols = data.shape[2]
    station = jnp.concatenate(
        [station_nodes[0].astype(f32).T, station_weights[0].T, station_counts.astype(f32),
         jnp.zeros((1, 128), f32)], axis=0)
    chips = parts // 2
    pay = packed(prior, station, chips)
    groups = [[2 * p + core for p in range(chips)] for core in range(2)]
    near = lax.all_to_all(pay, "tile", 0, 0, axis_index_groups=groups)
    far = lax.ppermute(near, "tile", [(i, i ^ 1) for i in range(parts)])
    x, send = factor(kappa, tau, near, far, modes[0].T, data[0], steps)
    received = lax.all_to_all(send, "tm", 0, 0)
    out, mean_logdet = reduced(rho, received, x)
    return (out[None, None], mean_logdet)


def solution(mesh):
    return jax.shard_map(
        body,
        mesh=mesh,
        in_specs=(
            P("tile", None),
            P("tm", "tile", None),
            P("tm", "tile", None),
            P("tm", "tile"),
            P("tm", None, None),
            P("tm", None, None),
            P("tile"),
            P("tile"),
            P("tile"),
        ),
        out_specs=(P("tm", "tile", None, None), P("tile")),
        check_vma=False,
    )
```

```python
import jax
import jax.numpy as jnp
from jax import lax
from jax.experimental import pallas as pl
from jax.experimental.pallas import tpu as pltpu
from jax.sharding import PartitionSpec as P

f32 = jnp.float32
bf16 = jnp.bfloat16
NN = ((1,), (0,))
NT = ((1,), (1,))
TN = ((0,), (0,))
SEG = 32


def dot(a, b, dims=NN, precision=lax.Precision.HIGHEST):
    return lax.dot_general(a, b, (dims, ((), ())), precision=precision, preferred_element_type=f32)


def split(v):
    high = v.astype(bf16)
    return high, (v - high.astype(f32)).astype(bf16)


def dot3(a, b, dims=NN):
    ah, al = split(a)
    bh, bl = split(b)
    left = jnp.concatenate([ah, ah, al], axis=dims[0][0])
    right = jnp.concatenate([bh, bl, bh], axis=dims[1][0])
    return lax.dot_general(left, right, (dims, ((), ())), preferred_element_type=f32)


def iotas():
    return (
        lax.broadcasted_iota(jnp.int32, (8, 128), 0),
        lax.broadcasted_iota(jnp.int32, (8, 128), 1),
    )


def row_of(v, k):
    return jnp.broadcast_to(v[k : k + 1, :], v.shape)


def eliminate(columns, panel):
    sub, _ = iotas()
    own = list(columns)
    dets = jnp.ones((8, 128), f32)
    for k in range(0, 8, 2):
        ca, cb = own[k], own[k + 1]
        paa, pab, pbb = row_of(ca, k), row_of(cb, k), row_of(cb, k + 1)
        det = paa * pbb - pab * pab
        inv = 1.0 / det
        on_a, on_b = sub == k, sub == k + 1
        both = on_a | on_b
        na = jnp.where(on_a, -pbb, jnp.where(on_b, pab, ca * pbb - cb * pab))
        nb = jnp.where(on_a, pab, jnp.where(on_b, -paa, cb * paa - ca * pab))
        dets = jnp.where(on_a, det, dets)

        def step(v):
            return jnp.where(both, 0.0, v) - (na * row_of(v, k) + nb * row_of(v, k + 1)) * inv

        own[k + 2 :] = [step(v) for v in own[k + 2 :]]
        panel = step(panel)
    return panel, dets


def downdate(columns, spread):
    t = [columns[k] * spread[k] for k in range(8)]
    return ((t[0] + t[1]) + (t[2] + t[3])) + ((t[4] + t[5]) + (t[6] + t[7]))


def inverse128(rows):
    sub, lane = iotas()
    rows = list(rows)
    logs = jnp.zeros((8, 128), f32)
    lower, scaled = [], []
    for b in range(16):
        start = 8 * b
        before = lane < start
        until = lane < start + 8
        pivots = until & jnp.logical_not(before)
        identity = jnp.where(lane - start == sub, 1.0, 0.0)
        columns = [[jnp.broadcast_to(rows[g][:, start + k : start + k + 1], (8, 128)) for k in range(8)]
                   for g in range(b, 16)]
        panel, dets = eliminate(columns[0], jnp.where(pivots, identity, rows[b]))
        logs = logs + jnp.log(dets)
        lower.append(jnp.where(before, rows[b], identity))
        scaled.append(jnp.where(until, panel, 0.0))
        spread = [row_of(panel, k) for k in range(8)]
        for g in range(b + 1, 16):
            rows[g] = jnp.where(pivots, 0.0, rows[g]) - downdate(columns[g - b], spread)
    return dot3(jnp.concatenate(lower, axis=0), jnp.concatenate(scaled, axis=0), TN), logs


def inverse32(rows):
    sub, lane = iotas()
    local = lane % SEG
    first = lane - local
    logs = jnp.zeros((8, 128), f32)
    rows = list(rows)
    for b in range(4):
        start = 8 * b
        pivots = (local >= start) & (local < start + 8)
        columns = [[jnp.take_along_axis(rows[g], first + (start + k), axis=1) for k in range(8)] for g in range(4)]
        panel, dets = eliminate(columns[b], jnp.where(pivots, jnp.where(local - start == sub, 1.0, 0.0), rows[b]))
        logs = logs + jnp.log(dets)
        spread = [row_of(panel, k) for k in range(8)]
        for g in range(4):
            if g != b:
                rows[g] = jnp.where(pivots, 0.0, rows[g]) - downdate(columns[g], spread)
        rows[b] = panel
    return rows, logs


def assemble(kappa, core, near_ref, far_ref, work_ref, strip_ref):
    chips = near_ref.shape[0]
    nodes = work_ref.shape[0]
    lane = lax.broadcasted_iota(jnp.int32, (32, 128), 1)
    tiles = nodes // 128
    for i in range(2 * chips):
        own = (core == 0) if i % 2 == 0 else (core == 1)
        part = kappa * jnp.where(own, near_ref[i // 2, :72, :], far_ref[i // 2, :72, :])
        shift = SEG * (i % 4)
        last = part[64:72]
        eighth = jnp.concatenate(
            [last if q == 0 else pltpu.roll(last, 128 - SEG * q, 1) for q in range(4)], axis=0)
        blocks = [part[:32], part[32:64], jnp.where(lane < SEG, eighth, 0.0)]
        bare = [jnp.where(lane < SEG, 0.0, part[:32]), part[32:64]]
        if shift:
            blocks = [pltpu.roll(v, shift, 1) for v in blocks]
            bare = [pltpu.roll(v, shift, 1) for v in bare]
        zero = jnp.zeros((32, 128), f32)
        rows = slice(32 * i, 32 * i + 32)

        def laid(pieces, ref):
            pieces = pieces + [zero] * (tiles - len(pieces))
            for c in range(tiles):
                at = (i // 4 + c) % tiles
                v = jnp.where(lane < shift, pieces[c - 1], pieces[c]) if shift else pieces[c]
                ref[rows, 128 * at : 128 * at + 128] = v

        laid(blocks, work_ref)
        laid(bare, strip_ref)

def factor_kernel(kappa_ref, tau_ref, near_ref, far_ref, modes_ref, data_ref, x_ref, send_ref,
                  work_ref, high_ref, low_ref, strip_ref):
    step = lax.axis_index("tm")
    ranks, nodes = modes_ref.shape
    cols = data_ref.shape[1]
    chips = near_ref.shape[0]
    parts = 2 * chips
    core = lax.axis_index("tile") % 2
    band = nodes // parts
    tiles = nodes // 128
    kappa = kappa_ref[0]
    tau = tau_ref[0]
    ids = lax.broadcasted_iota(jnp.int32, (nodes, 128), 0).astype(f32)
    for p in range(parts):
        s = (near_ref if p < chips else far_ref)[p % chips, 72:, :]
        n0, n1, n2, w0, w1, w2 = [s[i : i + 1] for i in range(6)]
        root = jnp.sqrt(s[6:7])
        same01 = n1 == n0
        same02 = n2 == n0
        same12 = (n2 == n1) & jnp.logical_not(same02)
        w0 = w0 + jnp.where(same01, w1, 0.0) + jnp.where(same02, w2, 0.0)
        w1 = w1 + jnp.where(same12, w2, 0.0)
        w0, w1, w2 = w0 * root, w1 * root, w2 * root
        h0, h1, h2 = [w.astype(bf16).astype(f32) for w in (w0, w1, w2)]
        m0, m1, m2 = ids == n0, ids == n1, ids == n2

        def place(a, b, c):
            return jnp.where(m0, a, jnp.where(m1, b, jnp.where(m2, c, 0.0))).astype(bf16)

        at = slice(p * 128, (p + 1) * 128)
        high_ref[:, at] = place(h0, h1, h2)
        low_ref[:, at] = place(w0 - h0, w1 - h1, w2 - h2)
    assemble(kappa, core, near_ref, far_ref, work_ref, strip_ref)
    half = nodes // 2
    one, two = slice(0, half), slice(half, nodes)
    for rs in (one, two):
        work_ref[rs, rs] = work_ref[rs, rs] + tau * dot(high_ref[rs, :], high_ref[rs, :], NT, None)
        cross = tau * dot(high_ref[rs, :], low_ref[rs, :], NT, None)
        work_ref[rs, rs] = work_ref[rs, rs] + cross
        strip_ref[rs, rs] = strip_ref[rs, rs] + cross
    gram = dot(
        jnp.concatenate([high_ref[one, :], high_ref[one, :], low_ref[one, :]], axis=1),
        jnp.concatenate([high_ref[two, :], low_ref[two, :], high_ref[two, :]], axis=1), NT, None)
    work_ref[one, two] = work_ref[one, two] + tau * gram
    strip_ref[one, two] = strip_ref[one, two] + tau * gram
    for a in range(tiles):
        for b in range(tiles):
            ra, rb = slice(128 * a, 128 * a + 128), slice(128 * b, 128 * b + 128)
            work_ref[rb, ra] = work_ref[rb, ra] + strip_ref[ra, rb].T
    work_ref[:, nodes : nodes + cols] = data_ref[...]
    basis = modes_ref[...]
    four = jnp.concatenate([basis] * (128 // ranks), axis=0)
    for c in range(tiles):
        rs = slice(128 * c, 128 * (c + 1))
        work_ref[rs, nodes + cols :] = four[:, rs].T
    width = nodes + cols + 128
    logs = jnp.zeros((8, 128), f32)
    for k in range(tiles):
        rs = slice(128 * k, 128 * (k + 1))
        inv, more = inverse128([work_ref[128 * k + 8 * g : 128 * k + 8 * g + 8, rs] for g in range(16)])
        logs = logs + more
        cs = slice(128 * (k + 1), width)
        solved = dot3(inv, work_ref[rs, cs])
        for a, b in ((0, 128 * k), (128 * (k + 1), nodes)):
            if b > a:
                work_ref[a:b, cs] = work_ref[a:b, cs] - dot3(work_ref[a:b, rs], solved)
        work_ref[rs, cs] = solved
    x = work_ref[:, nodes:]
    x_ref[...] = x
    grams = dot(basis, x)
    loads = grams[:, :cols]
    gram = grams[:, cols:]
    rows, more = inverse32([gram[8 * g : 8 * g + 8] for g in range(4)])
    odd = step % 2 == 1
    sub, lane = iotas()
    own = jnp.concatenate(rows, axis=0)
    scaled = dot(own[:, :ranks], loads)
    top = jnp.where(odd, loads, scaled)
    total = jnp.sum(logs, axis=0, keepdims=True) + jnp.where(odd, 0.0, jnp.sum(more, axis=0, keepdims=True))
    chosen = jnp.where(odd, gram, own)
    bottom = place_rows(chosen, 0)
    bottom = jnp.where((sub == 7) & (lane == 3 * SEG), jnp.broadcast_to(total[:, :1], (8, 128)), bottom)
    send_ref[:, :ranks, :] = jnp.broadcast_to(top[None], (send_ref.shape[0],) + top.shape)
    send_ref[:, ranks:, :] = jnp.broadcast_to(bottom[None], (send_ref.shape[0],) + bottom.shape)


def place_rows(tiled, slot):
    _, lane = iotas()
    out = tiled[:8]
    for q in range(4):
        out = jnp.where(lane // SEG == (q + slot) % 4, tiled[8 * q : 8 * q + 8], out)
    return out


def tile_rows(tile, mirrored):
    sub, lane = iotas()
    local = lane % SEG
    out = [jnp.take_along_axis(tile, local + SEG * q, axis=1) for q in range(4)]
    if mirrored:
        mirror = jnp.broadcast_to(out[0][0:1, 31:32], (8, 128))
        out[3] = jnp.where((sub == 7) & (local == 0), mirror, out[3])
    return jnp.concatenate(out, axis=0)


def line_kernel(rho_ref, recv_ref, send_ref, local_ref):
    line = lax.axis_index("tm") // 4
    rho = rho_ref[0]
    squared = rho * rho
    sub, lane = iotas()
    d0, m1, d2, m3 = [tile_rows(recv_ref[i, 32:, :], True) for i in range(4)]
    b0, l1, b2, l3 = [recv_ref[i, :32, :] for i in range(4)]
    m1, m3 = squared * m1, squared * m3
    middle = d2 - m1 - m3
    rows, logs = inverse32([middle[8 * g : 8 * g + 8] for g in range(4)])
    inv = jnp.concatenate(rows, axis=0)
    pqc = dot(inv[:, :SEG], jnp.concatenate([m1, m3, b2 + rho * (l1 + l3)], axis=1))
    local_ref[...] = pqc
    back = dot(jnp.concatenate([m1[:, :SEG], m3[:, :SEG]], axis=0), pqc)
    total = jnp.sum(logs, axis=0, keepdims=True)[:, :1]
    for i in range(4):
        total = total + recv_ref[i, 39:40, 3 * SEG : 3 * SEG + 1]
    slot = line // 2
    own = place_rows(d0 - m1 - back[:32, :128], slot)
    own = jnp.where((sub == 7) & (lane == SEG * ((3 + slot) % 4)), jnp.broadcast_to(total, (8, 128)), own)
    whole = jnp.concatenate([
        b0 + rho * l1 + back[:32, 256:],
        rho * l3 + back[32:, 256:],
        own,
        place_rows(m3 + back[32:, 128:256], slot),
        place_rows(back[32:, :128], slot),
        place_rows(back[:32, 128:256], slot),
    ], axis=0)
    send_ref[...] = jnp.broadcast_to(whole[None], send_ref.shape)


def reduce_kernel(rho_ref, line_ref, local_ref, recv_ref, x_ref, out_ref, ld_ref, r_ref):
    step = lax.axis_index("tm")
    rho = rho_ref[0]
    ranks = 32
    cols = out_ref.shape[1]
    sub, lane = iotas()
    seg = lane // SEG
    big_row = lax.broadcasted_iota(jnp.int32, (128, 128), 0) // SEG
    big_lane = lax.broadcasted_iota(jnp.int32, (128, 128), 1) // SEG
    diagonal = big_row == big_lane
    wide_lane = lax.broadcasted_iota(jnp.int32, (ranks, 128), 1) // SEG

    def blocks(packed):
        return jnp.where(diagonal, jnp.concatenate([packed] * 4, axis=0), 0.0)

    def unpack(row, odd, mirrored=False):
        tiles = [recv_ref[odd + 2 * s, row : row + 8, :] for s in range(4)]
        out = []
        for q in range(4):
            z = tiles[0]
            for s in range(1, 4):
                z = jnp.where(seg == (q + s) % 4, tiles[s], z)
            if q:
                z = pltpu.roll(z, 128 - SEG * q, 1)
            out.append(z)
        if mirrored:
            mirror = jnp.broadcast_to(out[0][0:1, :], (8, 128))
            mirror = pltpu.roll(mirror, 128 - 31, 1)
            out[3] = jnp.where((sub == 7) & (lane % SEG == 0), mirror, out[3])
        return jnp.concatenate(out, axis=0)

    def stack(row, odd):
        return jnp.concatenate([recv_ref[odd + 2 * s, row : row + ranks, :] for s in range(4)], axis=0)

    def later(packed, by=1):
        return pltpu.roll(packed, 128 - SEG * by, 1)

    def earlier(packed, by=1):
        return pltpu.roll(packed, SEG * by, 1)

    def later_rows(v, by=1):
        return jnp.concatenate([v[SEG * by :], v[: SEG * by]], axis=0)

    def earlier_rows(v, by=1):
        return jnp.concatenate([v[-SEG * by :], v[: -SEG * by]], axis=0)

    def two(a, u, b, v):
        both = jnp.concatenate([blocks(a), blocks(b)], axis=1)
        return dot(both, jnp.concatenate([u, v], axis=0))

    def invert(packed):
        rows, logs = inverse32([packed[8 * g : 8 * g + 8] for g in range(4)])
        return jnp.concatenate(rows, axis=0), logs

    odd_d = unpack(64, 1, True) - unpack(72, 0)
    odd_b = stack(0, 1) + stack(32, 0)
    d0 = unpack(64, 0, True) - jnp.where(wide_lane == 0, 0.0, earlier(unpack(72, 1)))
    b0 = stack(0, 0) + jnp.where(big_row == 0, 0.0, earlier_rows(stack(32, 1)))
    left, left_t = unpack(80, 0), unpack(88, 0)
    right = jnp.where(wide_lane == 3, 0.0, unpack(80, 1))
    right_t = jnp.where(wide_lane == 3, 0.0, unpack(88, 1))
    g1, logs = invert(odd_d)
    p1 = dot(g1, blocks(left))
    q1 = dot(g1, blocks(right_t))
    c1 = dot(blocks(g1), odd_b)
    d0 = d0 - dot(left_t, blocks(p1)) - earlier(dot(right, blocks(q1)))
    b0 = b0 + dot(blocks(left_t), c1) + earlier_rows(dot(blocks(right), c1))
    l0 = earlier(dot(right, blocks(p1)))
    r0 = dot(left_t, blocks(q1))
    weight = 0.5
    for by in (1, 2):
        g0, more = invert(d0)
        logs = logs + weight * more
        p0 = dot(g0, blocks(l0))
        q0 = dot(g0, blocks(r0))
        c0 = dot(blocks(g0), b0)
        d0 = d0 - dot(l0, blocks(earlier(q0, by))) - dot(r0, blocks(later(p0, by)))
        b0 = b0 + two(l0, earlier_rows(c0, by), r0, later_rows(c0, by))
        if by == 1:
            l0, r0 = dot(l0, blocks(earlier(p0))), dot(r0, blocks(later(q0)))
        weight = weight * 0.5
    g0, more = invert(d0)
    logs = logs + 2 * weight * more
    s0 = dot(blocks(g0), b0)
    s1 = c1 + two(p1, s0, q1, later_rows(s0))
    for s in range(4):
        r_ref[2 * s] = s0[SEG * s : SEG * s + SEG]
        r_ref[2 * s + 1] = s1[SEG * s : SEG * s + SEG]
    r_ref[8] = jnp.zeros((ranks, cols), f32)
    line = step // 4
    first, following = r_ref[line], r_ref[line + 1]

    def pair(a, b, u, v):
        both = jnp.where(wide_lane == 0, a, jnp.where(wide_lane == 1, b, 0.0))
        return dot(both, jnp.concatenate([u, v, u, v], axis=0))

    third = local_ref[:, 256:] + pair(local_ref[:, :128], local_ref[:, 128:256], first, following)
    m1, m3 = [tile_rows(line_ref[i, ranks:, :], True) for i in (1, 3)]
    ends = line_ref[1, :ranks, :] + line_ref[3, :ranks, :] + rho * pair(m1, m3, first + third, third + following)
    inv = tile_rows(line_ref[0, ranks:, :], True)
    at = step % 4
    around = jnp.where(
        at == 0, dot(inv[:, :SEG], first) - line_ref[0, :ranks, :],
        rho * jnp.where(at == 1, first + third, jnp.where(at == 2, ends, third + following)))
    out_ref[...] = x_ref[:, :cols] + dot(x_ref[:, cols : cols + ranks], around)
    total = jnp.sum(jnp.where(lane % SEG == 0, logs, 0.0))
    extra = jnp.zeros((8, 128), f32)
    for y in range(8):
        place = SEG * ((3 + y // 2) % 4)
        extra = extra + jnp.where((sub == 7) & (lane == place), recv_ref[y, 64:72, :], 0.0)
    ld_ref[0] = (total + jnp.sum(extra)) / (32.0 * out_ref.shape[0])


VMEM = pl.BlockSpec(memory_space=pltpu.VMEM)
SMEM = pl.BlockSpec(memory_space=pltpu.SMEM)


def pack_kernel(prior_ref, station_ref, out_ref):
    i = lax.axis_index("tile")
    nodes = prior_ref.shape[1]
    chips = out_ref.shape[0]
    _, lane = iotas()
    rolled = pltpu.roll(prior_ref[...], (nodes - SEG * i) % nodes, 1)
    far = rolled[:, 256:384]
    eighth = jnp.zeros((8, 128), f32)
    for q in range(4):
        v = far[8 * q : 8 * q + 8]
        eighth = jnp.where(lane // SEG == q, v if q == 0 else pltpu.roll(v, SEG * q, 1), eighth)
    whole = jnp.concatenate([rolled[:, :128], rolled[:, 128:256], eighth, station_ref[...]], axis=0)
    out_ref[...] = jnp.broadcast_to(whole[None], (chips,) + whole.shape)


def packed(prior, station, chips):
    return pl.pallas_call(
        pack_kernel,
        out_shape=jax.ShapeDtypeStruct((chips, 80, 128), f32),
        in_specs=[VMEM, VMEM],
        out_specs=VMEM,
        name="pack",
    )(prior, station)


def factor(kappa, tau, near, far, modes, data, steps):
    nodes, cols = data.shape
    parts = 2 * near.shape[0]
    return pl.pallas_call(
        factor_kernel,
        out_shape=(jax.ShapeDtypeStruct((nodes, cols + 128), f32), jax.ShapeDtypeStruct((steps, 40, 128), f32)),
        in_specs=[SMEM, SMEM, VMEM, VMEM, VMEM, VMEM],
        out_specs=(VMEM, VMEM),
        scratch_shapes=[
            pltpu.VMEM((nodes, nodes + cols + 128), f32),
            pltpu.VMEM((nodes, parts * 128), bf16),
            pltpu.VMEM((nodes, parts * 128), bf16),
            pltpu.VMEM((nodes, nodes), f32),
        ],
        name="factor",
    )(kappa, tau, near, far, modes, data)


def line_reduced(rho, received, lines):
    return pl.pallas_call(
        line_kernel,
        out_shape=(jax.ShapeDtypeStruct((lines, 96, 128), f32), jax.ShapeDtypeStruct((32, 384), f32)),
        in_specs=[SMEM, VMEM],
        out_specs=(VMEM, VMEM),
        name="line",
    )(rho, received)


def reduced(rho, line, local, received, x):
    nodes, cols = x.shape[0], received.shape[2]
    return pl.pallas_call(
        reduce_kernel,
        out_shape=(jax.ShapeDtypeStruct((nodes, cols), f32), jax.ShapeDtypeStruct((1,), f32)),
        in_specs=[SMEM, VMEM, VMEM, VMEM, VMEM],
        out_specs=(VMEM, SMEM),
        scratch_shapes=[pltpu.VMEM((received.shape[0] + 1, 32, cols), f32)],
        name="reduced",
    )(rho, line, local, received, x)


def body(prior, station_nodes, station_weights, station_counts, modes, data, kappa, tau, rho):
    parts = lax.axis_size("tile")
    steps = lax.axis_size("tm")
    band, nodes = prior.shape
    cols = data.shape[2]
    station = jnp.concatenate(
        [station_nodes[0].astype(f32).T, station_weights[0].T, station_counts.astype(f32),
         jnp.zeros((1, 128), f32)], axis=0)
    chips = parts // 2
    pay = packed(prior, station, chips)
    groups = [[2 * p + core for p in range(chips)] for core in range(2)]
    near = lax.all_to_all(pay, "tile", 0, 0, axis_index_groups=groups)
    far = lax.ppermute(near, "tile", [(i, i ^ 1) for i in range(parts)])
    lines = steps // 4
    along = [[4 * y + x for x in range(4)] for y in range(lines)]
    across = [[4 * y + x for y in range(lines)] for x in range(4)]
    x, send = factor(kappa, tau, near, far, modes[0].T, data[0], 4)
    line = lax.all_to_all(send, "tm", 0, 0, axis_index_groups=along)
    send, local = line_reduced(rho, line, lines)
    received = lax.all_to_all(send, "tm", 0, 0, axis_index_groups=across)
    out, mean_logdet = reduced(rho, line, local, received, x)
    return (out[None, None], mean_logdet)


def solution(mesh):
    return jax.shard_map(
        body,
        mesh=mesh,
        in_specs=(
            P("tile", None),
            P("tm", "tile", None),
            P("tm", "tile", None),
            P("tm", "tile"),
            P("tm", None, None),
            P("tm", None, None),
            P("tile"),
            P("tile"),
            P("tile"),
        ),
        out_specs=(P("tm", "tile", None, None), P("tile")),
        check_vma=False,
    )
```

```python
import jax
import jax.numpy as jnp
from jax import lax
from jax.experimental import pallas as pl
from jax.experimental.pallas import tpu as pltpu
from jax.sharding import PartitionSpec as P

f32 = jnp.float32
bf16 = jnp.bfloat16
NN = ((1,), (0,))
NT = ((1,), (1,))
TN = ((0,), (0,))
SEG = 32


def dot(a, b, dims=NN, precision=lax.Precision.HIGHEST):
    return lax.dot_general(a, b, (dims, ((), ())), precision=precision, preferred_element_type=f32)


def split(v):
    high = v.astype(bf16)
    return high, (v - high.astype(f32)).astype(bf16)


def dot3(a, b, dims=NN):
    ah, al = split(a)
    bh, bl = split(b)
    left = jnp.concatenate([ah, ah, al], axis=dims[0][0])
    right = jnp.concatenate([bh, bl, bh], axis=dims[1][0])
    return lax.dot_general(left, right, (dims, ((), ())), preferred_element_type=f32)


def iotas():
    return (
        lax.broadcasted_iota(jnp.int32, (8, 128), 0),
        lax.broadcasted_iota(jnp.int32, (8, 128), 1),
    )


def row_of(v, k):
    return jnp.broadcast_to(v[k : k + 1, :], v.shape)


def eliminate(columns, panel):
    sub, _ = iotas()
    own = list(columns)
    dets = jnp.ones((8, 128), f32)
    for k in range(0, 8, 2):
        ca, cb = own[k], own[k + 1]
        paa, pab, pbb = row_of(ca, k), row_of(cb, k), row_of(cb, k + 1)
        det = paa * pbb - pab * pab
        inv = 1.0 / det
        on_a, on_b = sub == k, sub == k + 1
        both = on_a | on_b
        na = jnp.where(on_a, -pbb, jnp.where(on_b, pab, ca * pbb - cb * pab))
        nb = jnp.where(on_a, pab, jnp.where(on_b, -paa, cb * paa - ca * pab))
        dets = jnp.where(on_a, det, dets)

        def step(v):
            return jnp.where(both, 0.0, v) - (na * row_of(v, k) + nb * row_of(v, k + 1)) * inv

        own[k + 2 :] = [step(v) for v in own[k + 2 :]]
        panel = step(panel)
    return panel, dets


def downdate(columns, spread):
    t = [columns[k] * spread[k] for k in range(8)]
    return ((t[0] + t[1]) + (t[2] + t[3])) + ((t[4] + t[5]) + (t[6] + t[7]))


def inverse128(rows):
    sub, lane = iotas()
    rows = list(rows)
    logs = jnp.zeros((8, 128), f32)
    lower, scaled = [], []
    for b in range(16):
        start = 8 * b
        before = lane < start
        until = lane < start + 8
        pivots = until & jnp.logical_not(before)
        identity = jnp.where(lane - start == sub, 1.0, 0.0)
        columns = [[jnp.broadcast_to(rows[g][:, start + k : start + k + 1], (8, 128)) for k in range(8)]
                   for g in range(b, 16)]
        panel, dets = eliminate(columns[0], jnp.where(pivots, identity, rows[b]))
        logs = logs + jnp.log(dets)
        lower.append(jnp.where(before, rows[b], identity))
        scaled.append(jnp.where(until, panel, 0.0))
        spread = [row_of(panel, k) for k in range(8)]
        for g in range(b + 1, 16):
            rows[g] = jnp.where(pivots, 0.0, rows[g]) - downdate(columns[g - b], spread)
    return dot3(jnp.concatenate(lower, axis=0), jnp.concatenate(scaled, axis=0), TN), logs


def inverse32(rows):
    sub, lane = iotas()
    local = lane % SEG
    first = lane - local
    logs = jnp.zeros((8, 128), f32)
    rows = list(rows)
    for b in range(4):
        start = 8 * b
        pivots = (local >= start) & (local < start + 8)
        columns = [[jnp.take_along_axis(rows[g], first + (start + k), axis=1) for k in range(8)] for g in range(4)]
        panel, dets = eliminate(columns[b], jnp.where(pivots, jnp.where(local - start == sub, 1.0, 0.0), rows[b]))
        logs = logs + jnp.log(dets)
        spread = [row_of(panel, k) for k in range(8)]
        for g in range(4):
            if g != b:
                rows[g] = jnp.where(pivots, 0.0, rows[g]) - downdate(columns[g], spread)
        rows[b] = panel
    return rows, logs


def assemble(kappa, core, near_ref, far_ref, work_ref, strip_ref):
    chips = near_ref.shape[0]
    nodes = work_ref.shape[0]
    lane = lax.broadcasted_iota(jnp.int32, (32, 128), 1)
    tiles = nodes // 128
    for i in range(2 * chips):
        own = (core == 0) if i % 2 == 0 else (core == 1)
        part = kappa * jnp.where(own, near_ref[i // 2, :72, :], far_ref[i // 2, :72, :])
        shift = SEG * (i % 4)
        last = part[64:72]
        eighth = jnp.concatenate(
            [last if q == 0 else pltpu.roll(last, 128 - SEG * q, 1) for q in range(4)], axis=0)
        blocks = [part[:32], part[32:64], jnp.where(lane < SEG, eighth, 0.0)]
        bare = [jnp.where(lane < SEG, 0.0, part[:32]), part[32:64]]
        if shift:
            blocks = [pltpu.roll(v, shift, 1) for v in blocks]
            bare = [pltpu.roll(v, shift, 1) for v in bare]
        zero = jnp.zeros((32, 128), f32)
        rows = slice(32 * i, 32 * i + 32)

        def laid(pieces, ref):
            pieces = pieces + [zero] * (tiles - len(pieces))
            for c in range(tiles):
                at = (i // 4 + c) % tiles
                v = jnp.where(lane < shift, pieces[c - 1], pieces[c]) if shift else pieces[c]
                ref[rows, 128 * at : 128 * at + 128] = v

        laid(blocks, work_ref)
        laid(bare, strip_ref)

def factor_kernel(kappa_ref, tau_ref, near_ref, far_ref, modes_ref, data_ref, x_ref, send_ref,
                  work_ref, high_ref, low_ref, strip_ref):
    step = lax.axis_index("tm")
    ranks, nodes = modes_ref.shape
    cols = data_ref.shape[1]
    chips = near_ref.shape[0]
    parts = 2 * chips
    core = lax.axis_index("tile") % 2
    band = nodes // parts
    tiles = nodes // 128
    kappa = kappa_ref[0]
    tau = tau_ref[0]
    ids = lax.broadcasted_iota(jnp.int32, (nodes, 128), 0).astype(f32)
    for p in range(parts):
        s = (near_ref if p < chips else far_ref)[p % chips, 72:, :]
        n0, n1, n2, w0, w1, w2 = [s[i : i + 1] for i in range(6)]
        root = jnp.sqrt(s[6:7])
        same01 = n1 == n0
        same02 = n2 == n0
        same12 = (n2 == n1) & jnp.logical_not(same02)
        w0 = w0 + jnp.where(same01, w1, 0.0) + jnp.where(same02, w2, 0.0)
        w1 = w1 + jnp.where(same12, w2, 0.0)
        w0, w1, w2 = w0 * root, w1 * root, w2 * root
        h0, h1, h2 = [w.astype(bf16).astype(f32) for w in (w0, w1, w2)]
        m0, m1, m2 = ids == n0, ids == n1, ids == n2

        def place(a, b, c):
            return jnp.where(m0, a, jnp.where(m1, b, jnp.where(m2, c, 0.0))).astype(bf16)

        at = slice(p * 128, (p + 1) * 128)
        high_ref[:, at] = place(h0, h1, h2)
        low_ref[:, at] = place(w0 - h0, w1 - h1, w2 - h2)
    assemble(kappa, core, near_ref, far_ref, work_ref, strip_ref)
    half = nodes // 2
    one, two = slice(0, half), slice(half, nodes)
    for rs in (one, two):
        work_ref[rs, rs] = work_ref[rs, rs] + tau * dot(high_ref[rs, :], high_ref[rs, :], NT, None)
        cross = tau * dot(high_ref[rs, :], low_ref[rs, :], NT, None)
        work_ref[rs, rs] = work_ref[rs, rs] + cross
        strip_ref[rs, rs] = strip_ref[rs, rs] + cross
    gram = dot(
        jnp.concatenate([high_ref[one, :], high_ref[one, :], low_ref[one, :]], axis=1),
        jnp.concatenate([high_ref[two, :], low_ref[two, :], high_ref[two, :]], axis=1), NT, None)
    work_ref[one, two] = work_ref[one, two] + tau * gram
    strip_ref[one, two] = strip_ref[one, two] + tau * gram
    for a in range(tiles):
        for b in range(tiles):
            ra, rb = slice(128 * a, 128 * a + 128), slice(128 * b, 128 * b + 128)
            work_ref[rb, ra] = work_ref[rb, ra] + strip_ref[ra, rb].T
    work_ref[:, nodes : nodes + cols] = data_ref[...]
    basis = modes_ref[...]
    four = jnp.concatenate([basis] * (128 // ranks), axis=0)
    for c in range(tiles):
        rs = slice(128 * c, 128 * (c + 1))
        work_ref[rs, nodes + cols :] = four[:, rs].T
    width = nodes + cols + 128
    logs = jnp.zeros((8, 128), f32)
    for k in range(tiles):
        rs = slice(128 * k, 128 * (k + 1))
        inv, more = inverse128([work_ref[128 * k + 8 * g : 128 * k + 8 * g + 8, rs] for g in range(16)])
        logs = logs + more
        cs = slice(128 * (k + 1), width)
        solved = dot3(inv, work_ref[rs, cs])
        for a, b in ((0, 128 * k), (128 * (k + 1), nodes)):
            if b > a:
                work_ref[a:b, cs] = work_ref[a:b, cs] - dot3(work_ref[a:b, rs], solved)
        work_ref[rs, cs] = solved
    x = work_ref[:, nodes:]
    x_ref[...] = x
    grams = dot(basis, x)
    loads = grams[:, :cols]
    gram = grams[:, cols:]
    rows, more = inverse32([gram[8 * g : 8 * g + 8] for g in range(4)])
    odd = step % 2 == 1
    sub, lane = iotas()
    own = jnp.concatenate(rows, axis=0)
    scaled = dot(own[:, :ranks], loads)
    top = jnp.where(odd, loads, scaled)
    total = jnp.sum(logs, axis=0, keepdims=True) + jnp.where(odd, 0.0, jnp.sum(more, axis=0, keepdims=True))
    chosen = jnp.where(odd, gram, own)
    bottom = place_rows(chosen, 0)
    bottom = jnp.where((sub == 7) & (lane == 3 * SEG), jnp.broadcast_to(total[:, :1], (8, 128)), bottom)
    send_ref[:, :ranks, :] = jnp.broadcast_to(top[None], (send_ref.shape[0],) + top.shape)
    send_ref[:, ranks:, :] = jnp.broadcast_to(bottom[None], (send_ref.shape[0],) + bottom.shape)


def place_rows(tiled, slot):
    _, lane = iotas()
    out = tiled[:8]
    for q in range(4):
        out = jnp.where(lane // SEG == (q + slot) % 4, tiled[8 * q : 8 * q + 8], out)
    return out


def tile_rows(tile, mirrored):
    sub, lane = iotas()
    local = lane % SEG
    out = [jnp.take_along_axis(tile, local + SEG * q, axis=1) for q in range(4)]
    if mirrored:
        mirror = jnp.broadcast_to(out[0][0:1, 31:32], (8, 128))
        out[3] = jnp.where((sub == 7) & (local == 0), mirror, out[3])
    return jnp.concatenate(out, axis=0)


def line_kernel(rho_ref, recv_ref, send_ref, local_ref):
    line = lax.axis_index("tm") // 4
    rho = rho_ref[0]
    squared = rho * rho
    sub, lane = iotas()
    d0, m1, d2, m3 = [tile_rows(recv_ref[i, 32:, :], True) for i in range(4)]
    b0, l1, b2, l3 = [recv_ref[i, :32, :] for i in range(4)]
    m1, m3 = squared * m1, squared * m3
    middle = d2 - m1 - m3
    rows, logs = inverse32([middle[8 * g : 8 * g + 8] for g in range(4)])
    inv = jnp.concatenate(rows, axis=0)
    pqc = dot(inv[:, :SEG], jnp.concatenate([m1, m3, b2 + rho * (l1 + l3)], axis=1))
    local_ref[...] = pqc
    back = dot(jnp.concatenate([m1[:, :SEG], m3[:, :SEG]], axis=0), pqc)
    total = jnp.sum(logs, axis=0, keepdims=True)[:, :1]
    for i in range(4):
        total = total + recv_ref[i, 39:40, 3 * SEG : 3 * SEG + 1]
    slot = line // 2
    own = place_rows(d0 - m1 - back[:32, :128], slot)
    own = jnp.where((sub == 7) & (lane == SEG * ((3 + slot) % 4)), jnp.broadcast_to(total, (8, 128)), own)
    whole = jnp.concatenate([
        b0 + rho * l1 + back[:32, 256:],
        rho * l3 + back[32:, 256:],
        own,
        place_rows(m3 + back[32:, 128:256], slot),
        place_rows(back[32:, :128], slot),
        place_rows(back[:32, 128:256], slot),
    ], axis=0)
    send_ref[...] = jnp.broadcast_to(whole[None], send_ref.shape)


def reduce_kernel(rho_ref, line_ref, local_ref, recv_ref, x_ref, out_ref, ld_ref, r_ref):
    step = lax.axis_index("tm")
    rho = rho_ref[0]
    ranks = 32
    cols = out_ref.shape[1]
    sub, lane = iotas()
    seg = lane // SEG
    big_row = lax.broadcasted_iota(jnp.int32, (128, 128), 0) // SEG
    big_lane = lax.broadcasted_iota(jnp.int32, (128, 128), 1) // SEG
    diagonal = big_row == big_lane
    wide_lane = lax.broadcasted_iota(jnp.int32, (ranks, 128), 1) // SEG

    def blocks(packed):
        return jnp.where(diagonal, jnp.concatenate([packed] * 4, axis=0), 0.0)

    def unpack(row, odd, mirrored=False):
        tiles = [recv_ref[odd + 2 * s, row : row + 8, :] for s in range(4)]
        out = []
        for q in range(4):
            z = tiles[0]
            for s in range(1, 4):
                z = jnp.where(seg == (q + s) % 4, tiles[s], z)
            if q:
                z = pltpu.roll(z, 128 - SEG * q, 1)
            out.append(z)
        if mirrored:
            mirror = jnp.broadcast_to(out[0][0:1, :], (8, 128))
            mirror = pltpu.roll(mirror, 128 - 31, 1)
            out[3] = jnp.where((sub == 7) & (lane % SEG == 0), mirror, out[3])
        return jnp.concatenate(out, axis=0)

    def stack(row, odd):
        return jnp.concatenate([recv_ref[odd + 2 * s, row : row + ranks, :] for s in range(4)], axis=0)

    def later(packed, by=1):
        return pltpu.roll(packed, 128 - SEG * by, 1)

    def earlier(packed, by=1):
        return pltpu.roll(packed, SEG * by, 1)

    def later_rows(v, by=1):
        return jnp.concatenate([v[SEG * by :], v[: SEG * by]], axis=0)

    def earlier_rows(v, by=1):
        return jnp.concatenate([v[-SEG * by :], v[: -SEG * by]], axis=0)

    def two(a, u, b, v):
        both = jnp.concatenate([blocks(a), blocks(b)], axis=1)
        return dot(both, jnp.concatenate([u, v], axis=0))

    def invert(packed):
        rows, logs = inverse32([packed[8 * g : 8 * g + 8] for g in range(4)])
        return jnp.concatenate(rows, axis=0), logs

    odd_d = unpack(64, 1, True) - unpack(72, 0)
    odd_b = stack(0, 1) + stack(32, 0)
    d0 = unpack(64, 0, True) - jnp.where(wide_lane == 0, 0.0, earlier(unpack(72, 1)))
    b0 = stack(0, 0) + jnp.where(big_row == 0, 0.0, earlier_rows(stack(32, 1)))
    left, left_t = unpack(80, 0), unpack(88, 0)
    right = jnp.where(wide_lane == 3, 0.0, unpack(80, 1))
    right_t = jnp.where(wide_lane == 3, 0.0, unpack(88, 1))
    g1, logs = invert(odd_d)
    p1 = dot(g1, blocks(left))
    q1 = dot(g1, blocks(right_t))
    c1 = dot(blocks(g1), odd_b)
    d0 = d0 - dot(left_t, blocks(p1)) - earlier(dot(right, blocks(q1)))
    b0 = b0 + dot(blocks(left_t), c1) + earlier_rows(dot(blocks(right), c1))
    l0 = earlier(dot(right, blocks(p1)))
    r0 = dot(left_t, blocks(q1))
    weight = 0.5
    for by in (1, 2):
        g0, more = invert(d0)
        logs = logs + weight * more
        p0 = dot(g0, blocks(l0))
        q0 = dot(g0, blocks(r0))
        c0 = dot(blocks(g0), b0)
        d0 = d0 - dot(l0, blocks(earlier(q0, by))) - dot(r0, blocks(later(p0, by)))
        b0 = b0 + two(l0, earlier_rows(c0, by), r0, later_rows(c0, by))
        if by == 1:
            l0, r0 = dot(l0, blocks(earlier(p0))), dot(r0, blocks(later(q0)))
        weight = weight * 0.5
    g0, more = invert(d0)
    logs = logs + 2 * weight * more
    s0 = dot(blocks(g0), b0)
    s1 = c1 + two(p1, s0, q1, later_rows(s0))
    for s in range(4):
        r_ref[2 * s] = s0[SEG * s : SEG * s + SEG]
        r_ref[2 * s + 1] = s1[SEG * s : SEG * s + SEG]
    r_ref[8] = jnp.zeros((ranks, cols), f32)
    line = step // 4
    first, following = r_ref[line], r_ref[line + 1]

    def pair(a, b, u, v):
        both = jnp.where(wide_lane == 0, a, jnp.where(wide_lane == 1, b, 0.0))
        return dot(both, jnp.concatenate([u, v, u, v], axis=0))

    third = local_ref[:, 256:] + pair(local_ref[:, :128], local_ref[:, 128:256], first, following)
    m1, m3 = [tile_rows(line_ref[i, ranks:, :], True) for i in (1, 3)]
    ends = line_ref[1, :ranks, :] + line_ref[3, :ranks, :] + rho * pair(m1, m3, first + third, third + following)
    inv = tile_rows(line_ref[0, ranks:, :], True)
    at = step % 4
    around = jnp.where(
        at == 0, dot(inv[:, :SEG], first) - line_ref[0, :ranks, :],
        rho * jnp.where(at == 1, first + third, jnp.where(at == 2, ends, third + following)))
    out_ref[...] = x_ref[:, :cols] + dot(x_ref[:, cols : cols + ranks], around)
    total = jnp.sum(jnp.where(lane % SEG == 0, logs, 0.0))
    extra = jnp.zeros((8, 128), f32)
    for y in range(8):
        place = SEG * ((3 + y // 2) % 4)
        extra = extra + jnp.where((sub == 7) & (lane == place), recv_ref[y, 64:72, :], 0.0)
    ld_ref[0] = (total + jnp.sum(extra)) / (32.0 * out_ref.shape[0])


VMEM = pl.BlockSpec(memory_space=pltpu.VMEM)
SMEM = pl.BlockSpec(memory_space=pltpu.SMEM)


def on_chip(v):
    return pltpu.with_memory_space_constraint(v, pltpu.MemorySpace.VMEM)


def pack_kernel(prior_ref, station_ref, out_ref):
    i = lax.axis_index("tile")
    nodes = prior_ref.shape[1]
    chips = out_ref.shape[0]
    _, lane = iotas()
    rolled = pltpu.roll(prior_ref[...], (nodes - SEG * i) % nodes, 1)
    far = rolled[:, 256:384]
    eighth = jnp.zeros((8, 128), f32)
    for q in range(4):
        v = far[8 * q : 8 * q + 8]
        eighth = jnp.where(lane // SEG == q, v if q == 0 else pltpu.roll(v, SEG * q, 1), eighth)
    whole = jnp.concatenate([rolled[:, :128], rolled[:, 128:256], eighth, station_ref[...]], axis=0)
    out_ref[...] = jnp.broadcast_to(whole[None], (chips,) + whole.shape)


def packed(prior, station, chips):
    return pl.pallas_call(
        pack_kernel,
        out_shape=pltpu.VMEM((chips, 80, 128), f32),
        in_specs=[VMEM, VMEM],
        out_specs=VMEM,
        name="pack",
    )(prior, station)


def factor(kappa, tau, near, far, modes, data, steps):
    nodes, cols = data.shape
    parts = 2 * near.shape[0]
    return pl.pallas_call(
        factor_kernel,
        out_shape=(pltpu.VMEM((nodes, cols + 128), f32), pltpu.VMEM((steps, 40, 128), f32)),
        in_specs=[SMEM, SMEM, VMEM, VMEM, VMEM, VMEM],
        out_specs=(VMEM, VMEM),
        scratch_shapes=[
            pltpu.VMEM((nodes, nodes + cols + 128), f32),
            pltpu.VMEM((nodes, parts * 128), bf16),
            pltpu.VMEM((nodes, parts * 128), bf16),
            pltpu.VMEM((nodes, nodes), f32),
        ],
        name="factor",
    )(kappa, tau, near, far, modes, data)


def line_reduced(rho, received, lines):
    return pl.pallas_call(
        line_kernel,
        out_shape=(pltpu.VMEM((lines, 96, 128), f32), pltpu.VMEM((32, 384), f32)),
        in_specs=[SMEM, VMEM],
        out_specs=(VMEM, VMEM),
        name="line",
    )(rho, received)


def reduced(rho, line, local, received, x):
    nodes, cols = x.shape[0], received.shape[2]
    return pl.pallas_call(
        reduce_kernel,
        out_shape=(jax.ShapeDtypeStruct((nodes, cols), f32), jax.ShapeDtypeStruct((1,), f32)),
        in_specs=[SMEM, VMEM, VMEM, VMEM, VMEM],
        out_specs=(VMEM, SMEM),
        scratch_shapes=[pltpu.VMEM((received.shape[0] + 1, 32, cols), f32)],
        name="reduced",
    )(rho, line, local, received, x)


def body(prior, station_nodes, station_weights, station_counts, modes, data, kappa, tau, rho):
    parts = lax.axis_size("tile")
    steps = lax.axis_size("tm")
    band, nodes = prior.shape
    cols = data.shape[2]
    station = jnp.concatenate(
        [station_nodes[0].astype(f32).T, station_weights[0].T, station_counts.astype(f32),
         jnp.zeros((1, 128), f32)], axis=0)
    chips = parts // 2
    pay = packed(prior, station, chips)
    groups = [[2 * p + core for p in range(chips)] for core in range(2)]
    near = lax.all_to_all(pay, "tile", 0, 0, axis_index_groups=groups)
    far = lax.ppermute(near, "tile", [(i, i ^ 1) for i in range(parts)])
    near, far = on_chip(near), on_chip(far)
    lines = steps // 4
    along = [[4 * y + x for x in range(4)] for y in range(lines)]
    across = [[4 * y + x for y in range(lines)] for x in range(4)]
    x, send = factor(kappa, tau, near, far, modes[0].T, data[0], 4)
    line = lax.all_to_all(send, "tm", 0, 0, axis_index_groups=along)
    line = on_chip(line)
    send, local = line_reduced(rho, line, lines)
    received = lax.all_to_all(send, "tm", 0, 0, axis_index_groups=across)
    out, mean_logdet = reduced(rho, line, on_chip(local), on_chip(received), on_chip(x))
    return (out[None, None], mean_logdet)


def solution(mesh):
    return jax.shard_map(
        body,
        mesh=mesh,
        in_specs=(
            P("tile", None),
            P("tm", "tile", None),
            P("tm", "tile", None),
            P("tm", "tile"),
            P("tm", None, None),
            P("tm", None, None),
            P("tile"),
            P("tile"),
            P("tile"),
        ),
        out_specs=(P("tm", "tile", None, None), P("tile")),
        check_vma=False,
    )
```
